32 devices in a mesh: tile: 16 (over z, x, core), case: 2 (over y).
Axes of the slice: x: 2, y: 2, z: 4, core: 2. Of those that a mesh axis runs over, the one named last changes fastest.
Arguments:
- load: float32 [4, 3, 24576], P('case', None, 'tile')
- target: float32 [4, 3, 24576], P('case', None, 'tile'), may hold values from -6 to 6
- lame_lambda: float32 [24576], P('tile'), may hold values from 0.5 to 2
- lame_mu: float32 [24576], P('tile'), may hold values from 0.5 to 2
- volume: float32 [24576], P('tile'), may hold values from 0.5 to 2
- smooth: float32 [192, 4, 3, 128, 128], P('tile'), may hold values from -0.25 to 0.25
- columns: int32 [192, 4], P('tile'), may hold values from 0 to 27, as said below
- send_list: int32 [16, 2, 8], P('tile'), may hold values from 0 to 11, as said below
- counts: int32 [16], P('tile'), may hold values from 192 to 1536, as said below
Outputs:
- displacement: float32 [4, 3, 24576], P('case', None, 'tile')
- grad_lambda: float32 [24576], P('tile')
- grad_mu: float32 [24576], P('tile')
The draws below stay inside these ranges and needn't reach their ends.
Inputs may be any that keep to these rules, and one draw needn't show every extreme that they name: `columns`: slot 0 of every block names the block itself (its index within the tile); in every tile, slot 3 of block 0 names pool block 12 and slot 3 of block 11 names pool block 27; the other slots name any block of the pool. Entries send_list[t, 1, 0] and send_list[t, 0, 7] are never 0. `counts`: some tile is full.
All inputs are finite; a program needn't handle non-finite values.
Results may differ from the reference program's by a relative error of at most 0.0001.
Values sent between devices are 32-bit elements; how exact they have to be, the bound alone decides.
No kernel may reach another device: no remote copies, remote signals or barrier semaphores. Data moves between devices by JAX's collectives and lax.ppermute only.
A program may use at most 64 MiB of HBM per device.

```python
import math
import jax
import jax.numpy as jnp
from jax import lax

NB = 12
PB = 128
K = 4
GMAX = 8
ITERS = 6
CASES = 4
BLOCKS = 192
PARTICLES = 24576
N_TILE = 16


def draw_load(key, part):
    ramp = 1.0 + 2.0 * jnp.arange(PARTICLES, dtype=jnp.float32) / PARTICLES
    base = jax.random.normal(key, (CASES, 3, PARTICLES), jnp.float32)
    return (base * ramp[None, None, :]).astype(jnp.float32)


def draw_columns(key, part):
    block_ids = jnp.arange(BLOCKS, dtype=jnp.int32) % NB
    others = jax.random.randint(key, (BLOCKS, K - 1), 0, NB + 2 * GMAX, dtype=jnp.int32)
    last_slot = others[:, K - 2]
    last_slot = jnp.where(block_ids == 0, NB, last_slot)
    last_slot = jnp.where(block_ids == NB - 1, NB + 2 * GMAX - 1, last_slot)
    others = jnp.concatenate([others[:, :K - 2], last_slot[:, None]], axis=1)
    return jnp.concatenate([block_ids[:, None], others], axis=1).astype(jnp.int32)


def draw_send_list(key, part):
    first, second, third = jax.random.split(jax.random.fold_in(key, 17), 3)
    lists = jax.random.randint(first, (N_TILE, 2, GMAX), 0, NB, dtype=jnp.int32)
    upper_first = jax.random.randint(second, (N_TILE,), 1, NB, dtype=jnp.int32)
    lower_last = jax.random.randint(third, (N_TILE,), 1, NB, dtype=jnp.int32)
    lists = lists.at[:, 1, 0].set(upper_first)
    lists = lists.at[:, 0, GMAX - 1].set(lower_last)
    return lists.astype(jnp.int32)


def draw_counts(key, part):
    first, second = jax.random.split(key)
    values = jax.random.randint(first, (N_TILE,), PB + PB // 2, NB * PB + 1, dtype=jnp.int32)
    chosen = jax.random.randint(second, (), 0, N_TILE, dtype=jnp.int32)
    return jnp.where(jnp.arange(N_TILE, dtype=jnp.int32) == chosen, NB * PB, values).astype(jnp.int32)


def block_scale(own_key, extent, shards, smallest, top_value):
    def one(dim, parts):
        steps = jax.random.uniform(jax.random.fold_in(jax.random.fold_in(own_key, 6), dim), (parts,), jnp.float32, smallest / len(shards), top_value / len(shards))
        return jnp.repeat(jnp.exp(steps), extent[dim] // parts).reshape((-1,) + (1,) * (len(extent) - dim - 1))

    gain = one(*shards[0])
    for cut in shards[1:]:
        gain = gain * one(*cut)
    return gain


def bell_draw(rng, shape, spread, limit, cuts=(), held_as=jnp.bfloat16):
    loudness = block_scale(rng, shape, cuts, -0.22, 0.18) if cuts else 1.0
    array = jax.random.normal(rng, shape, jnp.float32) * spread * loudness
    return jnp.minimum(jnp.maximum(array, -limit), limit).astype(held_as)


def setup_inputs(seed: int = 0) -> dict:
    key_of = jax.random.split(jax.random.key(seed), 10)
    load = draw_load(jax.random.fold_in(key_of[9], 71), 0)
    target = bell_draw(key_of[1], (CASES, 3, PARTICLES), 1.0, 6.0, ((0, 2), (2, 16)), jnp.float32)
    lame_lambda = jnp.clip(jnp.exp(math.log(2.0) - 1.3862944 * jax.random.uniform(key_of[2], (PARTICLES,), jnp.float32) ** block_scale(key_of[2], (PARTICLES,), ((0, 16),), -0.2, 0.2)), 0.5, 2.0)
    lame_mu = jnp.clip(jnp.exp(math.log(2.0) - 1.3862944 * jax.random.uniform(key_of[3], (PARTICLES,), jnp.float32) ** block_scale(key_of[3], (PARTICLES,), ((0, 16),), -0.2, 0.2)), 0.5, 2.0)
    volume = jnp.clip(jnp.exp(math.log(2.0) - 1.3862944 * jax.random.uniform(key_of[4], (PARTICLES,), jnp.float32) ** block_scale(key_of[4], (PARTICLES,), ((0, 16),), -0.2, 0.2)), 0.5, 2.0)
    smooth = bell_draw(key_of[5], (BLOCKS, K, 3, PB, PB), (K * PB) ** -0.5, 0.25, ((0, 16),), jnp.float32)
    columns = draw_columns(jax.random.fold_in(key_of[9], 71), 0)
    send_list = draw_send_list(jax.random.fold_in(key_of[9], 71), 0)
    counts = draw_counts(jax.random.fold_in(key_of[9], 71), 0)
    return {"load": load, "target": target, "lame_lambda": lame_lambda, "lame_mu": lame_mu, "volume": volume, "smooth": smooth, "columns": columns, "send_list": send_list, "counts": counts}


HIGH = lax.Precision.HIGHEST
KAPPA = 0.5


def reference(load, target, lame_lambda, lame_mu, volume, smooth, columns, send_list, counts):
    tiles = counts.shape[0]
    nblk = smooth.shape[0] // tiles
    width = smooth.shape[3]
    ghosts = send_list.shape[2]
    slots = smooth.shape[1]
    pool_n = nblk + 2 * ghosts
    cases = load.shape[0]
    field_shape = (cases, 3, tiles, nblk, width)
    position = jnp.arange(nblk * width, dtype=jnp.int32)
    alive = (position[None, :] < counts[:, None]).astype(jnp.float32).reshape(tiles, nblk, width)
    weight = volume.reshape(tiles, nblk, width) * alive
    lam_weight = weight * lame_lambda.reshape(tiles, nblk, width)
    shear_weight = weight * lame_mu.reshape(tiles, nblk, width)
    grid = smooth.reshape(tiles, nblk, slots, 3, width, width)
    column_hot = (columns.reshape(tiles, nblk, slots)[..., None] == jnp.arange(pool_n, dtype=jnp.int32)).astype(jnp.float32)
    left_hot = (send_list[:, 0, :, None] == jnp.arange(nblk, dtype=jnp.int32)).astype(jnp.float32)
    right_hot = (send_list[:, 1, :, None] == jnp.arange(nblk, dtype=jnp.int32)).astype(jnp.float32)
    identity = jnp.eye(3, dtype=jnp.float32)

    def collect(field):
        to_left = jnp.einsum('cetbj,tgb->cetgj', field, left_hot, precision=HIGH)
        to_right = jnp.einsum('cetbj,tgb->cetgj', field, right_hot, precision=HIGH)
        blank = jnp.zeros_like(to_left[:, :, :1])
        from_left = jnp.concatenate([blank, to_right[:, :, :-1]], axis=2)
        from_right = jnp.concatenate([to_left[:, :, 1:], blank], axis=2)
        return jnp.concatenate([field, from_left, from_right], axis=3)

    def strains(field):
        pooled = collect(field * alive)
        gathered = jnp.einsum('cetqj,tbkq->cetbkj', pooled, column_hot, precision=HIGH)
        return jnp.einsum('tbkdij,cetbkj->cedtbi', grid, gathered, precision=HIGH)

    def operate(field):
        grads = strains(field)
        trace_u = grads[:, 0, 0] + grads[:, 1, 1] + grads[:, 2, 2]
        strain = 0.5 * (grads + jnp.swapaxes(grads, 1, 2))
        stress = 2.0 * shear_weight * strain + (lam_weight * trace_u)[:, None, None] * identity[None, :, :, None, None, None]
        contrib = jnp.einsum('tbkdij,cedtbi->cetbkj', grid, stress, precision=HIGH)
        pooled = jnp.einsum('cetbkj,tbkq->cetqj', contrib, column_hot, precision=HIGH)
        own = pooled[:, :, :, :nblk]
        lower_part = pooled[:, :, :, nblk:nblk + ghosts]
        upper_part = pooled[:, :, :, nblk + ghosts:]
        blank = jnp.zeros_like(lower_part[:, :, :1])
        from_left = jnp.concatenate([blank, upper_part[:, :, :-1]], axis=2)
        from_right = jnp.concatenate([lower_part[:, :, 1:], blank], axis=2)
        returned = jnp.einsum('cetgj,tgb->cetbj', from_left, left_hot, precision=HIGH) + jnp.einsum('cetgj,tgb->cetbj', from_right, right_hot, precision=HIGH)
        return alive * (own + returned) + KAPPA * field

    def inner(first, second):
        return jnp.sum(first * second, axis=(1, 2, 3, 4))

    def widen(scalars):
        return scalars[:, None, None, None, None]

    def run_solver(rhs):
        solution = jnp.zeros_like(rhs)
        residual = rhs
        direction = rhs
        norm_now = inner(residual, residual)
        for sweep in range(ITERS):
            image = operate(direction)
            step_len = norm_now / inner(direction, image)
            solution = solution + widen(step_len) * direction
            residual = residual - widen(step_len) * image
            norm_next = inner(residual, residual)
            direction = residual + widen(norm_next / norm_now) * direction
            norm_now = norm_next
        return solution

    forward = run_solver(alive * load.reshape(field_shape))
    adjoint = run_solver(alive * (forward - target.reshape(field_shape)))
    grads_u = strains(forward)
    grads_a = strains(adjoint)
    trace_u = grads_u[:, 0, 0] + grads_u[:, 1, 1] + grads_u[:, 2, 2]
    trace_a = grads_a[:, 0, 0] + grads_a[:, 1, 1] + grads_a[:, 2, 2]
    strain_u = 0.5 * (grads_u + jnp.swapaxes(grads_u, 1, 2))
    strain_a = 0.5 * (grads_a + jnp.swapaxes(grads_a, 1, 2))
    grad_lambda = -weight * jnp.sum(trace_u * trace_a, axis=0)
    grad_mu = -2.0 * weight * jnp.sum(strain_u * strain_a, axis=(0, 1, 2))
    return (forward.reshape(load.shape), grad_lambda.reshape(-1), grad_mu.reshape(-1))
```

```python
import functools

import jax
import jax.numpy as jnp
from jax import lax
from jax.experimental import pallas as pl
from jax.experimental.pallas import tpu as pltpu
from jax.sharding import PartitionSpec as P

ITERS = 6
KAPPA = 0.5
ROWS = 8
LANES = 128
F32 = jnp.float32
BF16 = jnp.bfloat16
LIMIT = 24 * 1024 * 1024

VM = pl.BlockSpec(memory_space=pltpu.VMEM)
SM = pl.BlockSpec(memory_space=pltpu.SMEM)


def call(body, outs, ins, scratch=(), flops=0, nbytes=0):
    return pl.pallas_call(
        body,
        out_shape=outs,
        in_specs=ins,
        out_specs=jax.tree.map(lambda _: VM, outs),
        scratch_shapes=list(scratch),
        compiler_params=pltpu.CompilerParams(vmem_limit_bytes=LIMIT),
        cost_estimate=pl.CostEstimate(flops=flops, bytes_accessed=nbytes, transcendentals=0),
    )


def arr(*shape, dtype=F32):
    return jax.ShapeDtypeStruct(shape, dtype)


def lane_iota():
    return lax.broadcasted_iota(jnp.int32, (ROWS, LANES), 1)


def row_iota():
    return lax.broadcasted_iota(jnp.int32, (ROWS, LANES), 0)


def split3(x):
    hi = x.astype(BF16)
    rest = x - hi.astype(F32)
    mid = rest.astype(BF16)
    low = (rest - mid.astype(F32)).astype(BF16)
    return jnp.concatenate([hi, mid, low], axis=0)


def fold3(y):
    return y[:ROWS] + (y[ROWS : 2 * ROWS] + y[2 * ROWS : 3 * ROWS])


def component_masks():
    row = row_iota()
    comp = lax.rem(row, 3)
    live = row < 6
    return [(live & (comp == e)).astype(F32) for e in range(3)]


def shift_rows(x, by):
    by = by % ROWS
    return x if by == 0 else pltpu.roll(x, by, 0)


def symmetric(g, masks):
    out = []
    for d in range(3):
        total = g[d]
        for e in range(3):
            total = total + masks[e] * shift_rows(g[e], e - d)
        out.append(total)
    return out


def trace_at(g, d):
    return shift_rows(g[0], d) + shift_rows(g[1], d - 1) + shift_rows(g[2], d - 2)


def stress_of(g, shear, lam, masks):
    sym = symmetric(g, masks)
    return [shear * sym[d] + lam * (masks[d] * trace_at(g, d)) for d in range(3)]


def forward_block(b, cols, split_ref, hi_ref, lo_ref):
    total = None
    for kp in range(2):
        left = split_ref[cols[b, 2 * kp]]
        right = split_ref[cols[b, 2 * kp + 1]]
        both = jnp.concatenate([left, right], axis=1)
        for ref in (hi_ref, lo_ref):
            part = lax.dot_general(
                both, ref[b, kp], (((1,), (1,)), ((), ())), preferred_element_type=F32
            )
            total = part if total is None else total + part
    return total


def backward_block(b, cols, stress, hi_ref, lo_ref, q_ref):
    parts = split3(jnp.concatenate(stress, axis=1))
    for kp in range(2):
        out = jnp.dot(parts, hi_ref[b, kp], preferred_element_type=F32)
        out = out + jnp.dot(parts, lo_ref[b, kp], preferred_element_type=F32)
        out = fold3(out)
        for k in range(2):
            q = cols[b, 2 * kp + k]
            q_ref[q] = q_ref[q] + out[:, k * LANES : (k + 1) * LANES]


def put_dot(acc, lane, x):
    total = jnp.sum(x, axis=1, keepdims=True)
    return jnp.where(lane_iota() == lane, total, acc)


def over_components(x, masks):
    total = None
    for shift in (-2, -1, 0, 1, 2):
        moved = shift_rows(x, shift)
        for e in range(3):
            if 0 <= e - shift < 3:
                term = masks[e] * moved
                total = term if total is None else total + term
    return total


def pairs(j):
    return [j * (j + 1) // 2 + i for i in range(j + 1)]


def entry(i, j):
    i, j = min(i, j), max(i, j)
    return j * (j + 1) // 2 + i


NGRAM = ITERS * (ITERS + 1) // 2


class Meta:
    UP, DOWN, COUNT, UP_B, DOWN_B, COUNT_B, UP_A, DOWN_A, COUNT_A = 0, 8, 16, 17, 25, 33, 34, 42, 50
    SIZE = 51


def alive_of(meta, q, nblk, ghosts):
    if q < nblk:
        start, count = q * LANES, meta[Meta.COUNT]
    elif q < nblk + ghosts:
        start, count = meta[Meta.UP_B + q - nblk] * LANES, meta[Meta.COUNT_B]
    else:
        start, count = meta[Meta.DOWN_A + q - nblk - ghosts] * LANES, meta[Meta.COUNT_A]
    return (lane_iota() + start < count).astype(F32)


def convert_body(nblk, s_ref, hi_ref, lo_ref):
    for kp in range(2):
        for k in range(2):
            x = s_ref[0, 2 * kp + k].reshape(3 * LANES, LANES)
            hi = x.astype(BF16)
            hi_ref[0, kp, :, k * LANES : (k + 1) * LANES] = hi
            lo_ref[0, kp, :, k * LANES : (k + 1) * LANES] = (x - hi.astype(F32)).astype(BF16)


def convert(smooth):
    nblk = smooth.shape[0]
    shape = (nblk, 2, 3 * LANES, 2 * LANES)
    return pl.pallas_call(
        functools.partial(convert_body, nblk),
        grid=(nblk,),
        in_specs=[pl.BlockSpec((1, 4, 3, LANES, LANES), lambda b: (b, 0, 0, 0, 0))],
        out_specs=[pl.BlockSpec((1,) + shape[1:], lambda b: (b, 0, 0, 0))] * 2,
        out_shape=[arr(*shape, dtype=BF16)] * 2,
        compiler_params=pltpu.CompilerParams(vmem_limit_bytes=LIMIT),
        cost_estimate=pl.CostEstimate(
            flops=smooth.size * 3, bytes_accessed=smooth.size * 8, transcendentals=0
        ),
    )(smooth)


def prepare_body(nblk, ghosts, sends, counts, load, target, v_ref, t_ref, up_ref, down_ref):
    row = row_iota()
    zero = jnp.zeros((ROWS, LANES), F32)
    for b in range(nblk):
        mask = (lane_iota() + b * LANES < counts[0]).astype(F32)
        for src, dst in ((load, v_ref), (target, t_ref)):
            x = zero
            for c in range(2):
                for e in range(3):
                    x = jnp.where(row == 3 * c + e, src[c, e, b : b + 1, :], x)
            dst[b] = x * mask
    for side, ref in ((1, up_ref), (0, down_ref)):
        for g in range(ghosts):
            ref[g] = v_ref[sends[side, g]]
            ref[ghosts + g] = t_ref[sends[side, g]]
        meta = zero
        lane = lane_iota()
        for g in range(ghosts):
            meta = jnp.where(lane == Meta.UP + g, sends[1, g].astype(F32), meta)
            meta = jnp.where(lane == Meta.DOWN + g, sends[0, g].astype(F32), meta)
        meta = jnp.where(lane == Meta.COUNT, counts[0].astype(F32), meta)
        ref[2 * ghosts] = meta


def split_pool(v_ref, split_ref, pool_n):
    for q in range(pool_n):
        split_ref[q] = split3(v_ref[q])


def finish(nblk, ghosts, meta, q_ref, own_ref, up_ref, down_ref):
    own_ref[...] = q_ref[:nblk]
    up_ref[:ghosts] = q_ref[nblk + ghosts :]
    down_ref[:ghosts] = q_ref[nblk : nblk + ghosts]
    for g in range(ghosts):
        up_ref[ghosts + g] = q_ref[meta[Meta.UP + g]]
        down_ref[ghosts + g] = q_ref[meta[Meta.DOWN + g]]


def grads_and_spread(nblk, cols, hi_ref, lo_ref, split_ref, shear_ref, lam_ref, g_ref, q_ref, energy):
    masks = component_masks()
    if q_ref is not None:
        q_ref[...] = jnp.zeros_like(q_ref)

    def step(b, acc):
        full = fold3(forward_block(b, cols, split_ref, hi_ref, lo_ref))
        g_ref[b] = full
        g = [full[:, d * LANES : (d + 1) * LANES] for d in range(3)]
        stress = stress_of(g, shear_ref[b], lam_ref[b], masks)
        if energy:
            acc = acc + (stress[0] * g[0] + (stress[1] * g[1] + stress[2] * g[2]))
        if q_ref is not None:
            backward_block(b, cols, stress, hi_ref, lo_ref, q_ref)
        return acc

    return lax.fori_loop(0, nblk, step, jnp.zeros((ROWS, LANES), F32))


def first_body(nblk, ghosts, cols, meta, v_own, t_own, below, above, hi_ref, lo_ref, shear_ref, lam_ref,
               v_ref, t_ref, g_ref, gt_ref, own_ref, up_ref, down_ref, gram_ref, split_ref, split_t, q_ref):
    pool_n = nblk + 2 * ghosts
    v_ref[:nblk] = v_own[...]
    t_ref[:nblk] = t_own[...]
    for g in range(ghosts):
        v_ref[nblk + g] = jnp.where(meta[Meta.COUNT_B] > 0, below[g], 0.0)
        t_ref[nblk + g] = jnp.where(meta[Meta.COUNT_B] > 0, below[ghosts + g], 0.0)
        v_ref[nblk + ghosts + g] = jnp.where(meta[Meta.COUNT_A] > 0, above[g], 0.0)
        t_ref[nblk + ghosts + g] = jnp.where(meta[Meta.COUNT_A] > 0, above[ghosts + g], 0.0)
    split_pool(v_ref, split_ref, pool_n)
    split_pool(t_ref, split_t, pool_n)
    grads_and_spread(nblk, cols, hi_ref, lo_ref, split_ref, shear_ref, lam_ref, g_ref, q_ref, False)

    def step(b, acc):
        gt_ref[b] = fold3(forward_block(b, cols, split_t, hi_ref, lo_ref))
        return acc

    lax.fori_loop(0, nblk, step, 0)
    finish(nblk, ghosts, meta, q_ref, own_ref, up_ref, down_ref)
    total = jnp.zeros((ROWS, LANES), F32)
    for b in range(nblk):
        total = total + v_ref[b] * v_ref[b]
    gram_ref[...] = put_dot(jnp.zeros((ROWS, LANES), F32), 0, total)


def gather_image(nblk, ghosts, meta, own, up, down, below1, above1, below2, above2, f_ref, s_ref):
    f_ref[:nblk] = own[...]
    has_b = meta[Meta.COUNT_B] > 0
    has_a = meta[Meta.COUNT_A] > 0
    s_ref[...] = jnp.zeros_like(s_ref)
    for g in range(ghosts):
        i = meta[Meta.UP + g]
        f_ref[i] = f_ref[i] + jnp.where(has_a, above1[g], 0.0)
        i = meta[Meta.UP_B + g]
        s_ref[0, i] = s_ref[0, i] + down[g]
        i = meta[Meta.DOWN_A + g]
        s_ref[1, i] = s_ref[1, i] + up[g]
    for g in range(ghosts):
        i = meta[Meta.DOWN + g]
        f_ref[i] = f_ref[i] + jnp.where(has_b, below1[g], 0.0)
        i = meta[Meta.DOWN_B + g]
        s_ref[0, i] = s_ref[0, i] + below2[g]
        i = meta[Meta.UP_A + g]
        s_ref[1, i] = s_ref[1, i] + above2[g]
    for g in range(ghosts):
        f_ref[nblk + g] = below1[ghosts + g] + s_ref[0, meta[Meta.UP_B + g]]
        f_ref[nblk + ghosts + g] = above1[ghosts + g] + s_ref[1, meta[Meta.DOWN_A + g]]


def image_body(nblk, ghosts, meta, own, up, down, below1, above1, below2, above2, v_ref, gram_in,
               w_ref, gram_ref, f_ref, s_ref):
    gather_image(nblk, ghosts, meta, own, up, down, below1, above1, below2, above2, f_ref, s_ref)
    vw = jnp.zeros((ROWS, LANES), F32)
    ww = vw
    for q in range(nblk + 2 * ghosts):
        w = alive_of(meta, q, nblk, ghosts) * f_ref[q] + KAPPA * v_ref[q]
        w_ref[q] = w
        if q < nblk:
            vw = vw + v_ref[q] * w
            ww = ww + w * w
    gram_ref[...] = put_dot(put_dot(gram_in[...], 1, vw), 2, ww)


def interval_body(devices, parts, out_ref):
    masks = component_masks()
    total = parts[0]
    for i in range(1, devices):
        total = total + parts[i]
    total = over_components(total, masks)
    vv, vw, ww = (jnp.broadcast_to(total[:, i : i + 1], (ROWS, LANES)) for i in range(3))
    live = vv > 0.0
    vv = jnp.where(live, vv, 1.0)
    first = jnp.where(live, vw / vv - KAPPA, 1.0)
    second = jnp.where(live, ww / vv - 2 * KAPPA * (vw / vv) + KAPPA * KAPPA, 2.0)
    first = jnp.maximum(first, 1e-6)
    spread = jnp.maximum(second / (first * first) - 1.0, 0.0)
    root = 1.0 + jnp.sqrt(spread)
    width = 1.5 * first * root * root
    out_ref[0] = KAPPA + 0.5 * width
    out_ref[1] = 0.5 * width
    out_ref[2] = 1.0 / (0.5 * width)


def step_body(j, nblk, ghosts, direct, last, *refs):
    refs = list(refs)
    take = lambda n: [refs.pop(0) for _ in range(n)]
    cols, meta = take(2)
    if direct:
        (w_in,) = take(1)
    else:
        own, up, down, below1, above1, below2, above2 = take(7)
    basis = take(j)
    coef, gram_in, hi_ref, lo_ref, shear_ref, lam_ref = take(6)
    v_ref, g_ref, gram_ref = take(3)
    if not last:
        own_o, up_o, down_o = take(3)
    split_ref = take(1)[0]
    if not direct:
        f_ref, s_ref = take(2)
    q_ref = None if last else take(1)[0]
    pool_n = nblk + 2 * ghosts
    centre, inverse = coef[0], coef[2]
    if j > 1:
        inverse = 2.0 * inverse
    if not direct:
        gather_image(nblk, ghosts, meta, own, up, down, below1, above1, below2, above2, f_ref, s_ref)
    dots = [jnp.zeros((ROWS, LANES), F32) for _ in range(j + 1)]
    for q in range(pool_n):
        prev = basis[j - 1][q]
        if direct:
            w = w_in[q]
        else:
            w = alive_of(meta, q, nblk, ghosts) * f_ref[q] + KAPPA * prev
        v = (w - centre * prev) * inverse
        if j > 1:
            v = v - basis[j - 2][q]
        v_ref[q] = v
        split_ref[q] = split3(v)
        if q < nblk:
            for i in range(j):
                dots[i] = dots[i] + basis[i][q] * v
            dots[j] = dots[j] + v * v
    gram = gram_in[...]
    for i, lane in enumerate(pairs(j)):
        gram = put_dot(gram, lane, dots[i])
    energy = grads_and_spread(
        nblk, cols, hi_ref, lo_ref, split_ref, shear_ref, lam_ref, g_ref, q_ref, last
    )
    if last:
        gram = put_dot(gram, NGRAM, energy)
    else:
        finish(nblk, ghosts, meta, q_ref, own_o, up_o, down_o)
    gram_ref[...] = gram


def coefficients(devices, parts, coef):
    masks = component_masks()
    total = parts[0]
    for i in range(1, devices):
        total = total + parts[i]
    total = over_components(total, masks)
    pick = lambda i: jnp.broadcast_to(total[:, i : i + 1], (ROWS, LANES))
    g = {(i, j): pick(entry(i, j)) for i in range(ITERS) for j in range(ITERS)}
    centre, half = coef[0], coef[1]

    def image(p):
        out = [None] * (len(p) + 1)

        def add(i, x):
            out[i] = x if out[i] is None else out[i] + x

        for j, x in enumerate(p):
            add(j, centre * x)
            if j == 0:
                add(1, half * x)
            else:
                add(j + 1, 0.5 * half * x)
                add(j - 1, 0.5 * half * x)
        return out

    def times(table, x, i):
        out = None
        for j, y in enumerate(x):
            term = table[i, j] * y
            out = term if out is None else out + term
        return out

    def form(x, table, y):
        out = None
        for i, z in enumerate(x):
            term = z * times(table, y, i)
            out = term if out is None else out + term
        return out

    last = ITERS - 1
    energy = {}
    for j in range(last):
        for i in range(j, ITERS):
            value = centre * g[i, j]
            if j == 0:
                value = value + half * g[i, 1]
            else:
                value = value + 0.5 * half * (g[i, j + 1] + g[i, j - 1])
            energy[i, j] = energy[j, i] = value
    energy[last, last] = pick(NGRAM) + KAPPA * g[last, last]
    one = jnp.ones((ROWS, LANES), F32)
    r, p = [one], [one]
    rr = g[0, 0]
    u = None
    for sweep in range(ITERS):
        alpha = rr / form(p, energy, p)
        if u is None:
            u = [alpha * x for x in p]
        else:
            u = [(u[i] + alpha * x) if i < len(u) else alpha * x for i, x in enumerate(p)]
        if sweep < last:
            moved = image(p)
            r = [(r[i] - alpha * x) if i < len(r) else -(alpha * x) for i, x in enumerate(moved)]
            new = form(r, g, r)
            beta = new / rr
            p = [(x + beta * p[i]) if i < len(p) else x for i, x in enumerate(r)]
            rr = new
    work = dict(g)
    worst = one
    for j in range(ITERS):
        pivot = work[j, j]
        worst = jnp.minimum(worst, jnp.where(pivot > 0.0, pivot / g[j, j], 0.0))
        scale = 1.0 / pivot
        for a in range(j + 1, ITERS):
            for b in range(j + 1, a + 1):
                work[a, b] = work[a, b] - work[a, j] * work[b, j] * scale
    live = row_iota() < 6
    return [jnp.where(live, x, 0.0) for x in u], worst


def mix(weights, refs, q):
    total = weights[0] * refs[0][q]
    for w, ref in zip(weights[1:], refs[1:]):
        total = total + w * ref[q]
    return total


def middle_body(nblk, ghosts, devices, *refs):
    refs = list(refs)
    take = lambda n: [refs.pop(0) for _ in range(n)]
    cols, meta, parts, coef = take(4)
    basis, grads = take(ITERS), take(ITERS)
    t_ref, gt_ref, hi_ref, lo_ref, shear_ref, lam_ref = take(6)
    disp_ref, gu_ref, v_ref, g_ref, gram_ref, worst_ref, own_o, up_o, down_o, q_ref = take(10)
    u, worst = coefficients(devices, parts, coef)
    worst_ref[...] = worst
    total = jnp.zeros((ROWS, LANES), F32)
    for q in range(nblk + 2 * ghosts):
        x = mix(u, basis, q)
        v = x - t_ref[q]
        v_ref[q] = v
        if q < nblk:
            for c in range(2):
                for e in range(3):
                    disp_ref[c, e, q : q + 1, :] = x[3 * c + e : 3 * c + e + 1, :]
            total = total + v * v
    gram_ref[...] = put_dot(jnp.zeros((ROWS, LANES), F32), 0, total)
    masks = component_masks()
    q_ref[...] = jnp.zeros_like(q_ref)
    wide = [jnp.concatenate([x] * 3, axis=1) for x in u]

    def step(b, acc):
        full = mix(wide, grads, b)
        gu_ref[b] = full
        full = full - gt_ref[b]
        g_ref[b] = full
        g = [full[:, d * LANES : (d + 1) * LANES] for d in range(3)]
        stress = stress_of(g, shear_ref[b], lam_ref[b], masks)
        backward_block(b, cols, stress, hi_ref, lo_ref, q_ref)
        return acc

    lax.fori_loop(0, nblk, step, 0)
    finish(nblk, ghosts, meta, q_ref, own_o, up_o, down_o)


def final_body(nblk, devices, *refs):
    refs = list(refs)
    take = lambda n: [refs.pop(0) for _ in range(n)]
    parts, coef = take(2)
    grads = take(ITERS)
    gu_ref, weight_ref, worst_in, out_ref = take(4)
    u, worst = coefficients(devices, parts, coef)
    worst = jnp.minimum(worst, worst_in[...])
    row = row_iota()
    worst = jnp.where(row < 6, worst, 1.0)
    masks = component_masks()
    wide = [jnp.concatenate([x] * 3, axis=1) for x in u]
    for b in range(nblk):
        full = mix(wide, grads, b)
        a = [full[:, d * LANES : (d + 1) * LANES] for d in range(3)]
        full = gu_ref[b]
        f = [full[:, d * LANES : (d + 1) * LANES] for d in range(3)]
        traces = masks[0] * (trace_at(a, 0) * trace_at(f, 0))
        sa, sf = symmetric(a, masks), symmetric(f, masks)
        work = sa[0] * sf[0] + (sa[1] * sf[1] + sa[2] * sf[2])
        work = (masks[0] + masks[1] + masks[2]) * work
        w = weight_ref[b]
        out_ref[b : b + 1, :] = -w[:1] * jnp.sum(traces, axis=0, keepdims=True)
        out_ref[nblk + b : nblk + b + 1, :] = (-0.5 * w[:1]) * jnp.sum(work, axis=0, keepdims=True)
    out_ref[2 * nblk : 2 * nblk + ROWS, :] = worst


def shift(x, by, size):
    return lax.ppermute(x, "tile", [(i, (i + by) % size) for i in range(size)])


def everywhere(x, size):
    return lax.all_to_all(jnp.broadcast_to(x[None], (size,) + x.shape), "tile", 0, 0)


def shards(load, target, lame_lambda, lame_mu, volume, smooth, columns, send_list, counts):
    cases = load.shape[0]
    nblk = smooth.shape[0]
    ghosts = send_list.shape[2]
    pool_n = nblk + 2 * ghosts
    tiles = lax.axis_size("tile")
    me = lax.axis_index("tile")
    flat = (nblk, LANES)
    alive = (jnp.arange(nblk * LANES, dtype=jnp.int32) < counts[0]).astype(F32).reshape(flat)
    weight = volume.reshape(flat) * alive
    tall = lambda x: jnp.broadcast_to(x[:, None, :], (nblk, ROWS, LANES))
    lam = tall(weight * lame_lambda.reshape(flat))
    shear = tall(weight * lame_mu.reshape(flat))
    weight = tall(weight)
    hi, lo = convert(smooth)
    block = lambda n: arr(n, ROWS, LANES)
    wide = lambda n: arr(n, ROWS, 3 * LANES)
    tile8 = arr(ROWS, LANES)
    v_own, t_own, up, down = call(
        functools.partial(prepare_body, nblk, ghosts),
        [block(nblk), block(nblk), block(2 * ghosts + 1), block(2 * ghosts + 1)],
        [SM, SM, VM, VM],
    )(send_list[0], counts, load.reshape(cases, 3, nblk, LANES), target.reshape(cases, 3, nblk, LANES))
    below = shift(up, 1, tiles)
    above = shift(down, -1, tiles)
    below_meta = below[2 * ghosts, 0, : Meta.COUNT + 1].astype(jnp.int32)
    above_meta = above[2 * ghosts, 0, : Meta.COUNT + 1].astype(jnp.int32)
    last = jnp.arange(Meta.COUNT + 1) == Meta.COUNT
    below_meta = jnp.where(last & (me == 0), 0, below_meta)
    above_meta = jnp.where(last & (me == tiles - 1), 0, above_meta)
    meta = jnp.concatenate([send_list[0, 1], send_list[0, 0], counts, below_meta, above_meta])
    matrix_scratch = pltpu.VMEM((pool_n, 3 * ROWS, LANES), BF16)
    pool_scratch = pltpu.VMEM((pool_n, ROWS, LANES), F32)
    side_scratch = pltpu.VMEM((2, nblk, ROWS, LANES), F32)
    msgs = [block(nblk), block(2 * ghosts), block(2 * ghosts)]
    v0, t_pool, g0, gt, own, up, down, gram = call(
        functools.partial(first_body, nblk, ghosts),
        [block(pool_n), block(pool_n), wide(nblk), wide(nblk)] + msgs + [tile8],
        [SM, SM] + [VM] * 8,
        [matrix_scratch, matrix_scratch, pool_scratch],
    )(columns, meta, v_own, t_own, below, above, hi, lo, shear, lam)

    def exchange(up, down):
        return (
            shift(up, 1, tiles),
            shift(down, -1, tiles),
            jnp.where(me >= 2, shift(up[:ghosts], 2, tiles), 0.0),
            jnp.where(me < tiles - 2, shift(down[:ghosts], -2, tiles), 0.0),
        )

    w, moments = call(
        functools.partial(image_body, nblk, ghosts),
        [block(pool_n), tile8],
        [SM] + [VM] * 9,
        [pool_scratch, side_scratch],
    )(meta, own, up, down, *exchange(up, down), v0, gram)
    coef = call(functools.partial(interval_body, tiles), [block(3)], [VM])(everywhere(moments, tiles))[0]

    def advance(j, basis, gram, own=None, up=None, down=None, w=None):
        direct = w is not None
        final = j == ITERS - 1
        ins = [w] if direct else [own, up, down, *exchange(up, down)]
        ins += list(basis) + [coef, gram, hi, lo, shear, lam]
        scratch = [matrix_scratch]
        if not direct:
            scratch += [pool_scratch, side_scratch]
        if not final:
            scratch.append(pool_scratch)
        return call(
            functools.partial(step_body, j, nblk, ghosts, direct, final),
            [block(pool_n), wide(nblk), tile8] + ([] if final else msgs),
            [SM, SM] + [VM] * len(ins),
            scratch,
        )(columns, meta, *ins)

    basis, grads = [v0], [g0]
    for j in range(1, ITERS):
        if j == 1:
            v, g, gram, *rest = advance(j, basis, gram, w=w)
        else:
            v, g, gram, *rest = advance(j, basis, gram, *rest)
        basis.append(v)
        grads.append(g)
    disp, gu, v0, g0, gram, worst, *rest = call(
        functools.partial(middle_body, nblk, ghosts, tiles),
        [arr(cases, 3, nblk, LANES), wide(nblk), block(pool_n), wide(nblk), tile8, tile8] + msgs,
        [SM, SM] + [VM] * (2 + 2 * ITERS + 6),
        [pool_scratch],
    )(columns, meta, everywhere(gram, tiles), coef, *basis, *grads, t_pool, gt, hi, lo, shear, lam)
    basis, grads = [v0], [g0]
    for j in range(1, ITERS):
        v, g, gram, *rest = advance(j, basis, gram, *rest)
        basis.append(v)
        grads.append(g)
    out = call(
        functools.partial(final_body, nblk, tiles),
        [arr(2 * nblk + ROWS, LANES)],
        [VM] * (2 + ITERS + 3),
    )(everywhere(gram, tiles), coef, *grads, gu, weight, worst)[0]
    other = lax.ppermute(out, "case", [(0, 1), (1, 0)])
    both = out[: 2 * nblk] + other[: 2 * nblk]
    return disp.reshape(load.shape), both[:nblk].reshape(-1), both[nblk:].reshape(-1)


def solution(mesh):
    return jax.shard_map(
        shards,
        mesh=mesh,
        in_specs=(
            P("case", None, "tile"),
            P("case", None, "tile"),
            P("tile"),
            P("tile"),
            P("tile"),
            P("tile", None, None, None, None),
            P("tile", None),
            P("tile", None, None),
            P("tile"),
        ),
        out_specs=(P("case", None, "tile"), P("tile"), P("tile")),
        check_vma=False,
    )
```

```python
import functools

import jax
import jax.numpy as jnp
from jax import lax
from jax.experimental import pallas as pl
from jax.experimental.pallas import tpu as pltpu
from jax.sharding import PartitionSpec as P

ITERS = 6
KAPPA = 0.5
ROWS = 8
LANES = 128
F32 = jnp.float32
BF16 = jnp.bfloat16
LIMIT = 14 * 1024 * 1024

VM = pl.BlockSpec(memory_space=pltpu.VMEM)
SM = pl.BlockSpec(memory_space=pltpu.SMEM)


def call(body, outs, ins, scratch=(), flops=0, nbytes=0, limit=LIMIT):
    return pl.pallas_call(
        body,
        out_shape=outs,
        in_specs=ins,
        out_specs=jax.tree.map(lambda _: VM, outs),
        scratch_shapes=list(scratch),
        compiler_params=pltpu.CompilerParams(vmem_limit_bytes=limit),
        cost_estimate=pl.CostEstimate(flops=flops, bytes_accessed=nbytes, transcendentals=0),
    )


def arr(*shape, dtype=F32):
    return jax.ShapeDtypeStruct(shape, dtype)


def in_hbm(x):
    return pltpu.with_memory_space_constraint(x, pltpu.HBM)


def lane_iota():
    return lax.broadcasted_iota(jnp.int32, (ROWS, LANES), 1)


def row_iota():
    return lax.broadcasted_iota(jnp.int32, (ROWS, LANES), 0)


def split3(x):
    hi = x.astype(BF16)
    rest = x - hi.astype(F32)
    mid = rest.astype(BF16)
    low = (rest - mid.astype(F32)).astype(BF16)
    return jnp.concatenate([hi, mid, low], axis=0)


def fold3(y):
    return y[:ROWS] + (y[ROWS : 2 * ROWS] + y[2 * ROWS : 3 * ROWS])


def component_masks():
    row = row_iota()
    comp = lax.rem(row, 3)
    live = row < 6
    return [(live & (comp == e)).astype(F32) for e in range(3)]


def shift_rows(x, by):
    by = by % ROWS
    return x if by == 0 else pltpu.roll(x, by, 0)


def symmetric(g, masks):
    out = []
    for d in range(3):
        total = g[d]
        for e in range(3):
            total = total + masks[e] * shift_rows(g[e], e - d)
        out.append(total)
    return out


def trace_at(g, d):
    return shift_rows(g[0], d) + shift_rows(g[1], d - 1) + shift_rows(g[2], d - 2)


def stress_of(g, shear, lam, masks):
    sym = symmetric(g, masks)
    return [shear * sym[d] + lam * (masks[d] * trace_at(g, d)) for d in range(3)]


def forward_block(b, cols, split_refs, fwd_ref):
    sides = []
    for ref in split_refs:
        line = jnp.concatenate([ref[cols[b, k]] for k in range(4)], axis=1)
        sides.append(line)
    line = sides[0] if len(sides) == 1 else jnp.concatenate(sides, axis=0)
    out = jnp.dot(
        jnp.concatenate([line, line], axis=1), fwd_ref[b], preferred_element_type=F32
    )
    return [fold3(out[3 * ROWS * i : 3 * ROWS * (i + 1)]) for i in range(len(sides))]


def backward_block(b, cols, stress, bwd_ref, q_ref):
    parts = split3(jnp.concatenate(stress, axis=1))
    out = jnp.dot(
        jnp.concatenate([parts, parts], axis=1), bwd_ref[b], preferred_element_type=F32
    )
    out = fold3(out)
    for k in range(4):
        q = cols[b, k]
        q_ref[q] = q_ref[q] + out[:, k * LANES : (k + 1) * LANES]


def put_dot(acc, lane, x):
    total = jnp.sum(x, axis=1, keepdims=True)
    return jnp.where(lane_iota() == lane, total, acc)


def over_components(x, masks):
    total = None
    for shift in (-2, -1, 0, 1, 2):
        moved = shift_rows(x, shift)
        for e in range(3):
            if 0 <= e - shift < 3:
                term = masks[e] * moved
                total = term if total is None else total + term
    return total


def pairs(j):
    return [j * (j + 1) // 2 + i for i in range(j + 1)]


def entry(i, j):
    i, j = min(i, j), max(i, j)
    return j * (j + 1) // 2 + i


NGRAM = ITERS * (ITERS + 1) // 2


class Table:
    NUMBER = 5
    UP, DOWN, COUNT, SIZE = 0, 8, 16, 17

    def __init__(self, refs):
        self.place, self.sends, self.counts, self.below, self.above = refs
        self.core = lax.rem(self.place[0], 2)
        self.even = lax.rem(self.place[0], 4) < 2

    def up(self, g):
        return self.sends[0, 1, g]

    def down(self, g):
        return self.sends[0, 0, g]


def alive_of(table, q, nblk, ghosts):
    if q < nblk:
        start, count = q * LANES, table.counts[0]
    elif q < nblk + ghosts:
        start, count = table.below[Table.UP + q - nblk] * LANES, table.below[Table.COUNT]
    else:
        start, count = table.above[Table.DOWN + q - nblk - ghosts] * LANES, table.above[Table.COUNT]
    return (lane_iota() + start < count).astype(F32)


DEPTH = 4


def convert_body(nblk, s_hbm, fwd_ref, bwd_ref, buf, sem):
    def copy(b, slot):
        return pltpu.make_async_copy(s_hbm.at[b], buf.at[slot], sem.at[slot])

    for b in range(min(DEPTH, nblk)):
        copy(b, b).start()

    def step(b, carry):
        slot = lax.rem(b, DEPTH)
        copy(b, slot).wait()
        for k in range(4):
            for d in range(3):
                x = buf[slot, k, d]
                rows, lanes = slice(d * LANES, (d + 1) * LANES), slice(k * LANES, (k + 1) * LANES)
                for y, ref, first, second, size in (
                    (x, bwd_ref, rows, lanes, 3 * LANES),
                    (x.T, fwd_ref, lanes, rows, 4 * LANES),
                ):
                    hi = y.astype(BF16)
                    ref[b, first, second] = hi
                    ref[b, slice(first.start + size, first.stop + size), second] = (
                        y - hi.astype(F32)
                    ).astype(BF16)

        @pl.when(b + DEPTH < nblk)
        def _():
            copy(b + DEPTH, slot).start()

        return carry

    lax.fori_loop(0, nblk, step, 0)


def convert(smooth):
    nblk = smooth.shape[0]
    return call(
        functools.partial(convert_body, nblk),
        [
            arr(nblk, 8 * LANES, 3 * LANES, dtype=BF16),
            arr(nblk, 6 * LANES, 4 * LANES, dtype=BF16),
        ],
        [pl.BlockSpec(memory_space=pltpu.HBM)],
        [pltpu.VMEM((DEPTH,) + smooth.shape[1:], F32), pltpu.SemaphoreType.DMA((DEPTH,))],
        flops=smooth.size * 3,
        nbytes=smooth.size * 12,
    )(in_hbm(smooth))


def prepare_body(nblk, ghosts, place, sends, counts, *refs):
    sources, outs, scratch, sem = refs[:5], refs[5:13], refs[13:18], refs[18]
    copies = [pltpu.make_async_copy(x, y, sem.at[i]) for i, (x, y) in enumerate(zip(sources, scratch))]
    for copy in copies:
        copy.start()
    for copy in copies:
        copy.wait()
    load, target, lam, mu, volume = scratch
    v_ref, t_ref, up_ref, down_ref, lam_ref, shear_ref, weight_ref, mask_ref = outs
    row, lane = row_iota(), lane_iota()
    zero = jnp.zeros((ROWS, LANES), F32)
    for b in range(nblk):
        at = slice(b * LANES, (b + 1) * LANES)
        alive = (lane + b * LANES < counts[0]).astype(F32)
        for src, dst in ((load, v_ref), (target, t_ref)):
            x = zero
            for c in range(2):
                for e in range(3):
                    x = jnp.where(row == 3 * c + e, src[e, c : c + 1, at], x)
            dst[b] = x * alive
        tall = lambda x: jnp.broadcast_to(x[at].reshape(1, LANES), (ROWS, LANES))
        weight = tall(volume) * alive
        weight_ref[b] = weight
        lam_ref[b] = weight * tall(lam)
        shear_ref[b] = weight * tall(mu)
    meta = jnp.where(lane == Table.COUNT, counts[0].astype(F32), zero)
    for g in range(ghosts):
        meta = jnp.where(lane == Table.UP + g, sends[0, 1, g].astype(F32), meta)
        meta = jnp.where(lane == Table.DOWN + g, sends[0, 0, g].astype(F32), meta)
    for side, ref in ((1, up_ref), (0, down_ref)):
        for g in range(ghosts):
            ref[g] = v_ref[sends[0, side, g]]
            ref[ghosts + g] = t_ref[sends[0, side, g]]
        ref[2 * ghosts] = meta
    forward_first = (lax.rem(place[0], 4) < 2) == (lax.rem(place[0], 2) == 0)
    mask_ref[...] = jnp.where(forward_first, 1.0, zero)


def split_pool(v_ref, split_ref, pool_n):
    for q in range(pool_n):
        split_ref[q] = split3(v_ref[q])


def finish(nblk, ghosts, table, q_ref, own_ref, near_ref, first_ref, second_ref, ghost_ref):
    own_ref[...] = q_ref[:nblk]
    ghost_ref[...] = q_ref[nblk:]
    for g in range(2 * ghosts):
        if g < ghosts:
            up, down = q_ref[nblk + ghosts + g], q_ref[nblk + g]
        else:
            up, down = q_ref[table.up(g - ghosts)], q_ref[table.down(g - ghosts)]
        near_ref[g] = jnp.where(table.core == 0, up, down)
        first_ref[g] = jnp.where(table.even, up, down)
        second_ref[g] = jnp.where(table.even, down, up)


def grads_and_spread(nblk, cols, fwd_ref, bwd_ref, split_refs, shear_ref, lam_ref, g_refs, q_ref, energy):
    masks = component_masks()
    if q_ref is not None:
        q_ref[...] = jnp.zeros_like(q_ref)

    def use(b, full, acc):
        for ref, x in zip(g_refs, full):
            ref[b] = x
        if not energy and q_ref is None:
            return acc
        g = [full[0][:, d * LANES : (d + 1) * LANES] for d in range(3)]
        stress = stress_of(g, shear_ref[b], lam_ref[b], masks)
        if energy:
            acc = acc + (stress[0] * g[0] + (stress[1] * g[1] + stress[2] * g[2]))
        if q_ref is not None:
            backward_block(b, cols, stress, bwd_ref, q_ref)
        return acc

    def forward(b):
        return forward_block(b, cols, split_refs, fwd_ref)

    def step(i, carry):
        full, acc = carry
        after = forward(2 * i + 1)
        acc = use(2 * i, full, acc)
        full = forward(jnp.minimum(2 * i + 2, nblk - 1))
        acc = use(2 * i + 1, after, acc)
        return full, acc

    start = (forward(0), jnp.zeros((ROWS, LANES), F32))
    full, acc = lax.fori_loop(0, nblk // 2, step, start)
    if nblk % 2:
        acc = use(nblk - 1, full, acc)
    return acc


def first_body(nblk, ghosts, cols, *refs):
    table = Table(refs[: Table.NUMBER])
    v_own, t_own, below, above, fwd_ref, bwd_ref, shear_ref, lam_ref = refs[Table.NUMBER : Table.NUMBER + 8]
    refs = refs[Table.NUMBER + 8 :]
    v_ref, t_ref, g_ref, gt_ref = refs[:4]
    messages, gram_ref, (split_ref, split_t, q_ref) = refs[4:9], refs[9], refs[10:]
    pool_n = nblk + 2 * ghosts
    v_ref[:nblk] = v_own[...]
    t_ref[:nblk] = t_own[...]
    for g in range(ghosts):
        v_ref[nblk + g] = below[g]
        t_ref[nblk + g] = below[ghosts + g]
        v_ref[nblk + ghosts + g] = above[g]
        t_ref[nblk + ghosts + g] = above[ghosts + g]
    split_pool(v_ref, split_ref, pool_n)
    split_pool(t_ref, split_t, pool_n)
    grads_and_spread(
        nblk, cols, fwd_ref, bwd_ref, [split_ref, split_t], shear_ref, lam_ref, [g_ref, gt_ref], q_ref, False
    )
    finish(nblk, ghosts, table, q_ref, *messages)
    total = jnp.zeros((ROWS, LANES), F32)
    for b in range(nblk):
        total = total + v_ref[b] * v_ref[b]
    gram_ref[...] = put_dot(jnp.zeros((ROWS, LANES), F32), 0, total)


def gather_image(nblk, ghosts, table, own, ghost, near, relay, first, second, f_ref, s_ref):
    f_ref[:nblk] = own[...]
    s_ref[...] = jnp.zeros_like(s_ref)
    low = table.core == 0
    below1 = lambda g: jnp.where(low, relay[g], near[g])
    above1 = lambda g: jnp.where(low, near[g], relay[g])
    below2 = lambda g: jnp.where(table.even, second[g], first[g])
    above2 = lambda g: jnp.where(table.even, first[g], second[g])

    def add(ref, at, x):
        ref[at] = ref[at] + x

    for g in range(ghosts):
        add(f_ref, table.up(g), above1(g))
        add(s_ref.at[0], table.below[Table.UP + g], ghost[g])
        add(s_ref.at[1], table.above[Table.DOWN + g], ghost[ghosts + g])
    for g in range(ghosts):
        add(f_ref, table.down(g), below1(g))
        add(s_ref.at[0], table.below[Table.DOWN + g], below2(g))
        add(s_ref.at[1], table.above[Table.UP + g], above2(g))
    for g in range(ghosts):
        f_ref[nblk + g] = below1(ghosts + g) + s_ref[0, table.below[Table.UP + g]]
        f_ref[nblk + ghosts + g] = above1(ghosts + g) + s_ref[1, table.above[Table.DOWN + g]]


def pack_gram(gram):
    total = over_components(gram, component_masks())
    low = lax.broadcasted_iota(jnp.int32, (1, LANES), 1) < LANES // 2
    row = jnp.where(low, total[:1], pltpu.roll(total, LANES // 2, 1)[3:4])
    return jnp.broadcast_to(row, (ROWS, LANES))


def unpack_gram(devices, parts):
    total = parts[0]
    for i in range(1, devices):
        total = total + parts[i]
    total = jnp.where(row_iota() < 3, total, pltpu.roll(total, LANES // 2, 1))
    return lambda i: jnp.broadcast_to(total[:, i : i + 1], (ROWS, LANES))


def image_body(nblk, ghosts, *refs):
    table = Table(refs[: Table.NUMBER])
    refs = refs[Table.NUMBER :]
    v_ref, gram_in, w_ref, gram_ref, f_ref, s_ref = refs[6:]
    gather_image(nblk, ghosts, table, *refs[:6], f_ref, s_ref)
    vw = jnp.zeros((ROWS, LANES), F32)
    ww = vw
    for q in range(nblk + 2 * ghosts):
        w = alive_of(table, q, nblk, ghosts) * f_ref[q] + KAPPA * v_ref[q]
        w_ref[q] = w
        if q < nblk:
            vw = vw + v_ref[q] * w
            ww = ww + w * w
    gram_ref[...] = pack_gram(put_dot(put_dot(gram_in[...], 1, vw), 2, ww))


def interval_body(devices, parts, out_ref):
    pick = unpack_gram(devices, parts)
    vv, vw, ww = pick(0), pick(1), pick(2)
    live = vv > 0.0
    vv = jnp.where(live, vv, 1.0)
    first = jnp.where(live, vw / vv - KAPPA, 1.0)
    second = jnp.where(live, ww / vv - 2 * KAPPA * (vw / vv) + KAPPA * KAPPA, 2.0)
    first = jnp.maximum(first, 1e-6)
    spread = jnp.maximum(second / (first * first) - 1.0, 0.0)
    root = 1.0 + jnp.sqrt(spread)
    width = 1.5 * first * root * root
    out_ref[0] = KAPPA + 0.5 * width
    out_ref[1] = 0.5 * width
    out_ref[2] = 1.0 / (0.5 * width)


def step_body(j, nblk, ghosts, direct, last, *refs):
    refs = list(refs)
    take = lambda n: [refs.pop(0) for _ in range(n)]
    cols, table = take(1)[0], Table(take(Table.NUMBER))
    if direct:
        (w_in,) = take(1)
    else:
        image_refs = take(6)
    basis = take(j)
    coef, gram_in, fwd_ref, bwd_ref, shear_ref, lam_ref = take(6)
    v_ref, g_ref, gram_ref = take(3)
    if not last:
        messages = take(5)
    split_ref = take(1)[0]
    if not direct:
        f_ref, s_ref = take(2)
    q_ref = None if last else take(1)[0]
    pool_n = nblk + 2 * ghosts
    centre, inverse = coef[0], coef[2]
    if j > 1:
        inverse = 2.0 * inverse
    if not direct:
        gather_image(nblk, ghosts, table, *image_refs, f_ref, s_ref)
    dots = [jnp.zeros((ROWS, LANES), F32) for _ in range(j + 1)]
    for q in range(pool_n):
        prev = basis[j - 1][q]
        if direct:
            w = w_in[q]
        else:
            w = alive_of(table, q, nblk, ghosts) * f_ref[q] + KAPPA * prev
        v = (w - centre * prev) * inverse
        if j > 1:
            v = v - basis[j - 2][q]
        v_ref[q] = v
        split_ref[q] = split3(v)
        if q < nblk:
            for i in range(j):
                dots[i] = dots[i] + basis[i][q] * v
            dots[j] = dots[j] + v * v
    gram = gram_in[...]
    for i, lane in enumerate(pairs(j)):
        gram = put_dot(gram, lane, dots[i])
    energy = grads_and_spread(
        nblk, cols, fwd_ref, bwd_ref, [split_ref], shear_ref, lam_ref, [g_ref], q_ref, last
    )
    if last:
        gram_ref[...] = pack_gram(put_dot(gram, NGRAM, energy))
    else:
        finish(nblk, ghosts, table, q_ref, *messages)
        gram_ref[...] = gram


def coefficients(devices, parts, coef):
    pick = unpack_gram(devices, parts)
    g = {(i, j): pick(entry(i, j)) for i in range(ITERS) for j in range(ITERS)}
    centre, half = coef[0], coef[1]

    def image(p):
        out = [None] * (len(p) + 1)

        def add(i, x):
            out[i] = x if out[i] is None else out[i] + x

        for j, x in enumerate(p):
            add(j, centre * x)
            if j == 0:
                add(1, half * x)
            else:
                add(j + 1, 0.5 * half * x)
                add(j - 1, 0.5 * half * x)
        return out

    def times(table, x, i):
        out = None
        for j, y in enumerate(x):
            term = table[i, j] * y
            out = term if out is None else out + term
        return out

    def form(x, table, y):
        out = None
        for i, z in enumerate(x):
            term = z * times(table, y, i)
            out = term if out is None else out + term
        return out

    last = ITERS - 1
    energy = {}
    for j in range(last):
        for i in range(j, ITERS):
            value = centre * g[i, j]
            if j == 0:
                value = value + half * g[i, 1]
            else:
                value = value + 0.5 * half * (g[i, j + 1] + g[i, j - 1])
            energy[i, j] = energy[j, i] = value
    energy[last, last] = pick(NGRAM) + KAPPA * g[last, last]
    one = jnp.ones((ROWS, LANES), F32)
    r, p = [one], [one]
    rr = g[0, 0]
    u = None
    for sweep in range(ITERS):
        alpha = rr / form(p, energy, p)
        if u is None:
            u = [alpha * x for x in p]
        else:
            u = [(u[i] + alpha * x) if i < len(u) else alpha * x for i, x in enumerate(p)]
        if sweep < last:
            moved = image(p)
            r = [(r[i] - alpha * x) if i < len(r) else -(alpha * x) for i, x in enumerate(moved)]
            new = form(r, g, r)
            beta = new / rr
            p = [(x + beta * p[i]) if i < len(p) else x for i, x in enumerate(r)]
            rr = new
    work = dict(g)
    worst = one
    for j in range(ITERS):
        pivot = work[j, j]
        worst = jnp.minimum(worst, jnp.where(pivot > 0.0, pivot / g[j, j], 0.0))
        scale = 1.0 / pivot
        for a in range(j + 1, ITERS):
            for b in range(j + 1, a + 1):
                work[a, b] = work[a, b] - work[a, j] * work[b, j] * scale
    live = row_iota() < 6
    return [jnp.where(live, x, 0.0) for x in u], worst


def mix(weights, refs, q):
    total = weights[0] * refs[0][q]
    for w, ref in zip(weights[1:], refs[1:]):
        total = total + w * ref[q]
    return total


def middle_body(nblk, ghosts, devices, *refs):
    refs = list(refs)
    take = lambda n: [refs.pop(0) for _ in range(n)]
    cols, table = take(1)[0], Table(take(Table.NUMBER))
    parts, coef = take(2)
    basis, grads = take(ITERS), take(ITERS)
    t_ref, gt_ref, fwd_ref, bwd_ref, shear_ref, lam_ref = take(6)
    disp_ref, gu_ref, v_ref, g_ref, gram_ref, worst_ref = take(6)
    messages, q_ref = take(5), take(1)[0]
    u, worst = coefficients(devices, parts, coef)
    worst_ref[...] = worst
    total = jnp.zeros((ROWS, LANES), F32)
    for q in range(nblk + 2 * ghosts):
        x = mix(u, basis, q)
        v = x - t_ref[q]
        v_ref[q] = v
        if q < nblk:
            for c in range(2):
                for e in range(3):
                    disp_ref[e, c : c + 1, q * LANES : (q + 1) * LANES] = x[3 * c + e : 3 * c + e + 1, :]
            total = total + v * v
    gram_ref[...] = put_dot(jnp.zeros((ROWS, LANES), F32), 0, total)
    masks = component_masks()
    q_ref[...] = jnp.zeros_like(q_ref)
    wide = [jnp.concatenate([x] * 3, axis=1) for x in u]

    def step(b, acc):
        full = mix(wide, grads, b)
        gu_ref[b] = full
        full = full - gt_ref[b]
        g_ref[b] = full
        g = [full[:, d * LANES : (d + 1) * LANES] for d in range(3)]
        stress = stress_of(g, shear_ref[b], lam_ref[b], masks)
        backward_block(b, cols, stress, bwd_ref, q_ref)
        return acc

    lax.fori_loop(0, nblk, step, 0)
    finish(nblk, ghosts, table, q_ref, *messages)


def final_body(nblk, devices, *refs):
    refs = list(refs)
    take = lambda n: [refs.pop(0) for _ in range(n)]
    parts, coef = take(2)
    grads = take(ITERS)
    gu_ref, weight_ref, worst_in, out_ref = take(4)
    u, worst = coefficients(devices, parts, coef)
    worst = jnp.minimum(worst, worst_in[...])
    row = row_iota()
    worst = jnp.where(row < 6, worst, 1.0)
    masks = component_masks()
    wide = [jnp.concatenate([x] * 3, axis=1) for x in u]
    for b in range(nblk):
        full = mix(wide, grads, b)
        a = [full[:, d * LANES : (d + 1) * LANES] for d in range(3)]
        full = gu_ref[b]
        f = [full[:, d * LANES : (d + 1) * LANES] for d in range(3)]
        traces = masks[0] * (trace_at(a, 0) * trace_at(f, 0))
        sa, sf = symmetric(a, masks), symmetric(f, masks)
        work = sa[0] * sf[0] + (sa[1] * sf[1] + sa[2] * sf[2])
        work = (masks[0] + masks[1] + masks[2]) * work
        w = weight_ref[b]
        out_ref[b : b + 1, :] = -w[:1] * jnp.sum(traces, axis=0, keepdims=True)
        out_ref[nblk + b : nblk + b + 1, :] = (-0.5 * w[:1]) * jnp.sum(work, axis=0, keepdims=True)
    out_ref[2 * nblk : 2 * nblk + ROWS, :] = worst


def pairs_of(step, offset, size):
    out = []
    for t in range(size):
        u = t - offset
        if u >= 0 and u % (2 * step) < step and t + step < size:
            out += [(t, t + step), (t + step, t)]
    return out


def everywhere(x, size):
    return lax.all_to_all(jnp.broadcast_to(x[None], (size,) + x.shape), "tile", 0, 0)


def shards(load, target, lame_lambda, lame_mu, volume, smooth, columns, send_list, counts):
    cases = load.shape[0]
    nblk = smooth.shape[0]
    ghosts = send_list.shape[2]
    pool_n = nblk + 2 * ghosts
    tiles, size = lax.axis_size("tile"), load.shape[2]
    place = lax.axis_index("tile").astype(jnp.int32).reshape(1)
    block = lambda n: arr(n, ROWS, LANES)
    wide = lambda n: arr(n, ROWS, 3 * LANES)
    tile8 = arr(ROWS, LANES)
    v_own, t_own, up, down, lam, shear, weight, mask = call(
        functools.partial(prepare_body, nblk, ghosts),
        [block(nblk)] * 2 + [block(2 * ghosts + 1)] * 2 + [block(nblk)] * 3 + [tile8],
        [SM] * 3 + [pl.BlockSpec(memory_space=pltpu.HBM)] * 5,
        [pltpu.VMEM(x, F32) for x in ((3, cases, size), (3, cases, size), (size,), (size,), (size,))]
        + [pltpu.SemaphoreType.DMA((5,))],
    )(
        place, send_list, counts, in_hbm(load.transpose(1, 0, 2)), in_hbm(target.transpose(1, 0, 2)),
        in_hbm(lame_lambda), in_hbm(lame_mu), in_hbm(volume),
    )
    below = lax.ppermute(up, "tile", [(t, t + 1) for t in range(tiles - 1)])
    above = lax.ppermute(down, "tile", [(t + 1, t) for t in range(tiles - 1)])
    fwd, bwd = convert(smooth)
    numbers = lambda x: x[2 * ghosts, 0, : Table.SIZE].astype(jnp.int32)
    table = (place, send_list, counts, numbers(below), numbers(above))
    matrix_scratch = pltpu.VMEM((pool_n, 3 * ROWS, LANES), BF16)
    pool_scratch = pltpu.VMEM((pool_n, ROWS, LANES), F32)
    side_scratch = pltpu.VMEM((2, nblk, ROWS, LANES), F32)
    msgs = [block(nblk)] + [block(2 * ghosts)] * 4
    scalars = [SM] * Table.NUMBER
    v0, t_pool, g0, gt, *rest, gram = call(
        functools.partial(first_body, nblk, ghosts),
        [block(pool_n)] * 2 + [wide(nblk)] * 2 + msgs + [tile8],
        [SM] + scalars + [VM] * 8,
        [matrix_scratch, matrix_scratch, pool_scratch],
    )(columns, *table, v_own, t_own, below, above, fwd, bwd, shear, lam)

    def exchange(own, near, first, second, ghost):
        near = lax.ppermute(near, "tile", pairs_of(1, 0, tiles))
        first = lax.ppermute(first, "tile", pairs_of(2, 0, tiles))
        second = lax.ppermute(second, "tile", pairs_of(2, 2, tiles))
        relay = lax.ppermute(jnp.where(mask > 0.0, first, second), "tile", pairs_of(1, 0, tiles))
        return own, ghost, near, relay, first, second

    w, moments = call(
        functools.partial(image_body, nblk, ghosts),
        [block(pool_n), tile8],
        scalars + [VM] * 8,
        [pool_scratch, side_scratch],
    )(*table, *exchange(*rest), v0, gram)
    coef = call(functools.partial(interval_body, tiles), [block(3)], [VM])(everywhere(moments, tiles))[0]

    def advance(j, basis, gram, rest, w=None):
        direct = w is not None
        final = j == ITERS - 1
        ins = [w] if direct else list(exchange(*rest))
        ins += list(basis) + [coef, gram, fwd, bwd, shear, lam]
        scratch = [matrix_scratch]
        if not direct:
            scratch += [pool_scratch, side_scratch]
        if not final:
            scratch.append(pool_scratch)
        return call(
            functools.partial(step_body, j, nblk, ghosts, direct, final),
            [block(pool_n), wide(nblk)] + ([tile8] if final else [tile8] + msgs),
            [SM] + scalars + [VM] * len(ins),
            scratch,
        )(columns, *table, *ins)

    basis, grads = [v0], [g0]
    for j in range(1, ITERS):
        v, g, gram, *rest = advance(j, basis, gram, rest, w if j == 1 else None)
        basis.append(v)
        grads.append(g)
    disp, gu, v0, g0, gram, worst, *rest = call(
        functools.partial(middle_body, nblk, ghosts, tiles),
        [arr(3, cases, size), wide(nblk), block(pool_n), wide(nblk), tile8, tile8] + msgs,
        [SM] + scalars + [VM] * (2 + 2 * ITERS + 6),
        [pool_scratch],
    )(columns, *table, everywhere(gram, tiles), coef, *basis, *grads, t_pool, gt, fwd, bwd, shear, lam)
    basis, grads = [v0], [g0]
    for j in range(1, ITERS):
        v, g, gram, *rest = advance(j, basis, gram, rest)
        basis.append(v)
        grads.append(g)
    out = call(
        functools.partial(final_body, nblk, tiles),
        [arr(2 * nblk + ROWS, LANES)],
        [VM] * (2 + ITERS + 3),
    )(everywhere(gram, tiles), coef, *grads, gu, weight, worst)[0]
    other = lax.ppermute(out, "case", [(0, 1), (1, 0)])
    both = out[: 2 * nblk] + other[: 2 * nblk]
    return disp.transpose(1, 0, 2), both[:nblk].reshape(-1), both[nblk:].reshape(-1)


def solution(mesh):
    return jax.shard_map(
        shards,
        mesh=mesh,
        in_specs=(
            P("case", None, "tile"),
            P("case", None, "tile"),
            P("tile"),
            P("tile"),
            P("tile"),
            P("tile", None, None, None, None),
            P("tile", None),
            P("tile", None, None),
            P("tile"),
        ),
        out_specs=(P("case", None, "tile"), P("tile"), P("tile")),
        check_vma=False,
    )
```

```python
import functools

import jax
import jax.numpy as jnp
from jax import lax
from jax.experimental import pallas as pl
from jax.experimental.pallas import tpu as pltpu
from jax.sharding import PartitionSpec as P

ITERS = 6
KAPPA = 0.5
CONDITION = 4000.0
SPAN = 7.2
ROWS = 8
LANES = 128
F32 = jnp.float32
BF16 = jnp.bfloat16
LIMIT = 14 * 1024 * 1024

VM = pl.BlockSpec(memory_space=pltpu.VMEM)
SM = pl.BlockSpec(memory_space=pltpu.SMEM)


def call(body, outs, ins, scratch=(), flops=0, nbytes=0, limit=LIMIT):
    return pl.pallas_call(
        body,
        out_shape=outs,
        in_specs=ins,
        out_specs=jax.tree.map(lambda _: VM, outs),
        scratch_shapes=list(scratch),
        compiler_params=pltpu.CompilerParams(vmem_limit_bytes=limit),
        cost_estimate=pl.CostEstimate(flops=flops, bytes_accessed=nbytes, transcendentals=0),
    )


def arr(*shape, dtype=F32):
    return jax.ShapeDtypeStruct(shape, dtype)


def in_hbm(x):
    return pltpu.with_memory_space_constraint(x, pltpu.HBM)


def lane_iota():
    return lax.broadcasted_iota(jnp.int32, (ROWS, LANES), 1)


def row_iota():
    return lax.broadcasted_iota(jnp.int32, (ROWS, LANES), 0)


def split3(x):
    hi = x.astype(BF16)
    rest = x - hi.astype(F32)
    mid = rest.astype(BF16)
    low = (rest - mid.astype(F32)).astype(BF16)
    return jnp.concatenate([hi, mid, low], axis=0)


def fold3(y):
    return y[:ROWS] + (y[ROWS : 2 * ROWS] + y[2 * ROWS : 3 * ROWS])


def component_masks():
    row = row_iota()
    comp = lax.rem(row, 3)
    live = row < 6
    return [(live & (comp == e)).astype(F32) for e in range(3)]


def shift_rows(x, by):
    by = by % ROWS
    return x if by == 0 else pltpu.roll(x, by, 0)


def symmetric(g, masks):
    out = []
    for d in range(3):
        total = g[d]
        for e in range(3):
            total = total + masks[e] * shift_rows(g[e], e - d)
        out.append(total)
    return out


def trace_at(g, d):
    return shift_rows(g[0], d) + shift_rows(g[1], d - 1) + shift_rows(g[2], d - 2)


def stress_of(g, shear, lam, masks):
    sym = symmetric(g, masks)
    return [shear * sym[d] + lam * (masks[d] * trace_at(g, d)) for d in range(3)]


def forward_block(b, cols, split_refs, fwd_ref):
    sides = []
    for ref in split_refs:
        line = jnp.concatenate([ref[cols[b, k]] for k in range(4)], axis=1)
        sides.append(line)
    line = sides[0] if len(sides) == 1 else jnp.concatenate(sides, axis=0)
    out = jnp.dot(
        jnp.concatenate([line, line], axis=1), fwd_ref[b], preferred_element_type=F32
    )
    return [fold3(out[3 * ROWS * i : 3 * ROWS * (i + 1)]) for i in range(len(sides))]


def backward_block(b, cols, stress, bwd_ref, q_ref):
    parts = split3(jnp.concatenate(stress, axis=1))
    out = jnp.dot(
        jnp.concatenate([parts, parts], axis=1), bwd_ref[b], preferred_element_type=F32
    )
    out = fold3(out)
    for k in range(4):
        q = cols[b, k]
        q_ref[q] = q_ref[q] + out[:, k * LANES : (k + 1) * LANES]


def put_dot(acc, lane, x):
    total = jnp.sum(x, axis=1, keepdims=True)
    return jnp.where(lane_iota() == lane, total, acc)


def over_components(x, masks):
    total = None
    for shift in (-2, -1, 0, 1, 2):
        moved = shift_rows(x, shift)
        for e in range(3):
            if 0 <= e - shift < 3:
                term = masks[e] * moved
                total = term if total is None else total + term
    return total


def pairs(j):
    return [j * (j + 1) // 2 + i for i in range(j + 1)]


def entry(i, j):
    i, j = min(i, j), max(i, j)
    return j * (j + 1) // 2 + i


NGRAM = ITERS * (ITERS + 1) // 2


class Table:
    NUMBER = 5
    UP, DOWN, COUNT, SIZE = 0, 8, 16, 17

    def __init__(self, refs):
        self.place, self.sends, self.counts, self.below, self.above = refs
        self.core = lax.rem(self.place[0], 2)
        self.even = lax.rem(self.place[0], 4) < 2

    def up(self, g):
        return self.sends[0, 1, g]

    def down(self, g):
        return self.sends[0, 0, g]


def alive_of(table, q, nblk, ghosts):
    if q < nblk:
        start, count = q * LANES, table.counts[0]
    elif q < nblk + ghosts:
        start, count = table.below[Table.UP + q - nblk] * LANES, table.below[Table.COUNT]
    else:
        start, count = table.above[Table.DOWN + q - nblk - ghosts] * LANES, table.above[Table.COUNT]
    return (lane_iota() + start < count).astype(F32)


DEPTH = 4


def convert_body(nblk, s_hbm, after, fwd_ref, bwd_ref, buf, sem):
    def copy(b, slot):
        return pltpu.make_async_copy(s_hbm.at[b], buf.at[slot], sem.at[slot])

    for b in range(min(DEPTH, nblk)):
        copy(b, b).start()

    def step(b, carry):
        slot = lax.rem(b, DEPTH)
        copy(b, slot).wait()
        for k in range(4):
            for d in range(3):
                x = buf[slot, k, d]
                rows, lanes = slice(d * LANES, (d + 1) * LANES), slice(k * LANES, (k + 1) * LANES)
                for y, ref, first, second, size in (
                    (x, bwd_ref, rows, lanes, 3 * LANES),
                    (x.T, fwd_ref, lanes, rows, 4 * LANES),
                ):
                    hi = y.astype(BF16)
                    ref[b, first, second] = hi
                    ref[b, slice(first.start + size, first.stop + size), second] = (
                        y - hi.astype(F32)
                    ).astype(BF16)

        @pl.when(b + DEPTH < nblk)
        def _():
            copy(b + DEPTH, slot).start()

        return carry

    lax.fori_loop(0, nblk, step, 0)


def convert(smooth, after):
    nblk = smooth.shape[0]
    return call(
        functools.partial(convert_body, nblk),
        [
            arr(nblk, 8 * LANES, 3 * LANES, dtype=BF16),
            arr(nblk, 6 * LANES, 4 * LANES, dtype=BF16),
        ],
        [pl.BlockSpec(memory_space=pltpu.HBM), VM],
        [pltpu.VMEM((DEPTH,) + smooth.shape[1:], F32), pltpu.SemaphoreType.DMA((DEPTH,))],
        flops=smooth.size * 3,
        nbytes=smooth.size * 12,
    )(in_hbm(smooth), after)


def prepare_body(nblk, ghosts, place, sends, counts, *refs):
    sources, outs, scratch, sem = refs[:6], refs[6:15], refs[15:21], refs[21]
    nrows = nblk * LANES
    copies = [pltpu.make_async_copy(x, y, sem.at[i]) for i, (x, y) in enumerate(zip((*sources[:5], sources[5].at[0, :2]), scratch))]
    for copy in copies:
        copy.start()
    for copy in copies:
        copy.wait()
    load, target, lam, mu, volume, piece = scratch
    v_ref, t_ref, up_ref, down_ref, lam_ref, shear_ref, weight_ref, mask_ref, sample_ref = outs
    row, lane = row_iota(), lane_iota()
    zero = jnp.zeros((ROWS, LANES), F32)
    for b in range(nblk):
        at = slice(b * LANES, (b + 1) * LANES)
        alive = (lane + b * LANES < counts[0]).astype(F32)
        for src, dst in ((load, v_ref), (target, t_ref)):
            x = zero
            for c in range(2):
                for e in range(3):
                    x = jnp.where(row == 3 * c + e, src[e, c : c + 1, at], x)
            dst[b] = x * alive
        tall = lambda x: jnp.broadcast_to(x[at].reshape(1, LANES), (ROWS, LANES))
        weight = tall(volume) * alive
        weight_ref[b] = weight
        lam_ref[b] = weight * tall(lam)
        shear_ref[b] = weight * tall(mu)
    meta = jnp.where(lane == Table.COUNT, counts[0].astype(F32), zero)
    for g in range(ghosts):
        meta = jnp.where(lane == Table.UP + g, sends[0, 1, g].astype(F32), meta)
        meta = jnp.where(lane == Table.DOWN + g, sends[0, 0, g].astype(F32), meta)
    for side, ref in ((1, up_ref), (0, down_ref)):
        for g in range(ghosts):
            ref[g] = v_ref[sends[0, side, g]]
            ref[ghosts + g] = t_ref[sends[0, side, g]]
        ref[2 * ghosts] = meta
    forward_first = (lax.rem(place[0], 4) < 2) == (lax.rem(place[0], 2) == 0)
    mask_ref[...] = jnp.where(forward_first, 1.0, zero)
    square = piece[0, 0] * piece[0, 0]
    for k in range(2):
        for d in range(3):
            if k + d > 0:
                square = square + piece[k, d] * piece[k, d]
    factor = 4.0 * shear_ref[0] + lam_ref[0]
    total = jnp.dot(factor, square, preferred_element_type=F32)
    total = jnp.sum(total, axis=1, keepdims=True) * (2.0 / (3 * LANES))
    share = counts[0].astype(F32) * (1.0 / nrows)
    sample_ref[...] = jnp.where(lane == 0, total, jnp.where(lane == 1, share, jnp.where(lane == 2, 1.0, 0.0)))


def split_pool(v_ref, split_ref, pool_n):
    for q in range(pool_n):
        split_ref[q] = split3(v_ref[q])


def finish(nblk, ghosts, table, q_ref, own_ref, near_ref, first_ref, second_ref, ghost_ref):
    own_ref[...] = q_ref[:nblk]
    ghost_ref[...] = q_ref[nblk:]
    for g in range(2 * ghosts):
        if g < ghosts:
            up, down = q_ref[nblk + ghosts + g], q_ref[nblk + g]
        else:
            up, down = q_ref[table.up(g - ghosts)], q_ref[table.down(g - ghosts)]
        near_ref[g] = jnp.where(table.core == 0, up, down)
        first_ref[g] = jnp.where(table.even, up, down)
        second_ref[g] = jnp.where(table.even, down, up)


def grads_and_spread(nblk, cols, fwd_ref, bwd_ref, split_refs, shear_ref, lam_ref, g_refs, q_ref, energy):
    masks = component_masks()
    if q_ref is not None:
        q_ref[...] = jnp.zeros_like(q_ref)

    def use(b, full, acc):
        for ref, x in zip(g_refs, full):
            ref[b] = x
        if not energy and q_ref is None:
            return acc
        g = [full[0][:, d * LANES : (d + 1) * LANES] for d in range(3)]
        stress = stress_of(g, shear_ref[b], lam_ref[b], masks)
        if energy:
            acc = acc + (stress[0] * g[0] + (stress[1] * g[1] + stress[2] * g[2]))
        if q_ref is not None:
            backward_block(b, cols, stress, bwd_ref, q_ref)
        return acc

    def forward(b):
        return forward_block(b, cols, split_refs, fwd_ref)

    def step(i, carry):
        full, acc = carry
        after = forward(2 * i + 1)
        acc = use(2 * i, full, acc)
        full = forward(jnp.minimum(2 * i + 2, nblk - 1))
        acc = use(2 * i + 1, after, acc)
        return full, acc

    start = (forward(0), jnp.zeros((ROWS, LANES), F32))
    full, acc = lax.fori_loop(0, nblk // 2, step, start)
    if nblk % 2:
        acc = use(nblk - 1, full, acc)
    return acc


def first_body(nblk, ghosts, cols, *refs):
    table = Table(refs[: Table.NUMBER])
    v_own, t_own, below, above, fwd_ref, bwd_ref, shear_ref, lam_ref, _ = refs[Table.NUMBER : Table.NUMBER + 9]
    refs = refs[Table.NUMBER + 9 :]
    v_ref, t_ref, g_ref, gt_ref = refs[:4]
    messages, gram_ref, (split_ref, split_t, q_ref) = refs[4:9], refs[9], refs[10:]
    pool_n = nblk + 2 * ghosts
    v_ref[:nblk] = v_own[...]
    t_ref[:nblk] = t_own[...]
    for g in range(ghosts):
        v_ref[nblk + g] = below[g]
        t_ref[nblk + g] = below[ghosts + g]
        v_ref[nblk + ghosts + g] = above[g]
        t_ref[nblk + ghosts + g] = above[ghosts + g]
    split_pool(v_ref, split_ref, pool_n)
    split_pool(t_ref, split_t, pool_n)
    grads_and_spread(
        nblk, cols, fwd_ref, bwd_ref, [split_ref, split_t], shear_ref, lam_ref, [g_ref, gt_ref], q_ref, False
    )
    finish(nblk, ghosts, table, q_ref, *messages)
    total = jnp.zeros((ROWS, LANES), F32)
    for b in range(nblk):
        total = total + v_ref[b] * v_ref[b]
    gram_ref[...] = put_dot(jnp.zeros((ROWS, LANES), F32), 0, total)


def gather_image(nblk, ghosts, table, own, ghost, near, relay, first, second, f_ref, lo_ref, hi_ref):
    f_ref[:nblk] = own[...]
    lo_ref[...] = jnp.zeros_like(lo_ref)
    hi_ref[...] = jnp.zeros_like(hi_ref)
    low = table.core == 0
    below1 = lambda g: jnp.where(low, relay[g], near[g])
    above1 = lambda g: jnp.where(low, near[g], relay[g])
    below2 = lambda g: jnp.where(table.even, second[g], first[g])
    above2 = lambda g: jnp.where(table.even, first[g], second[g])

    def add(ref, at, x):
        ref[at] = ref[at] + x

    for g in range(ghosts):
        add(f_ref, table.up(g), above1(g))
        add(lo_ref, table.below[Table.UP + g], ghost[g])
        add(hi_ref, table.above[Table.DOWN + g], ghost[ghosts + g])
    for g in range(ghosts):
        add(f_ref, table.down(g), below1(g))
        add(lo_ref, table.below[Table.DOWN + g], below2(g))
        add(hi_ref, table.above[Table.UP + g], above2(g))
    for g in range(ghosts):
        f_ref[nblk + g] = below1(ghosts + g) + lo_ref[table.below[Table.UP + g]]
        f_ref[nblk + ghosts + g] = above1(ghosts + g) + hi_ref[table.above[Table.DOWN + g]]


def pack_gram(gram):
    total = over_components(gram, component_masks())
    low = lax.broadcasted_iota(jnp.int32, (1, LANES), 1) < LANES // 2
    row = jnp.where(low, total[:1], pltpu.roll(total, LANES // 2, 1)[3:4])
    return jnp.broadcast_to(row, (ROWS, LANES))


def unpack_gram(devices, parts):
    total = parts[0]
    for i in range(1, devices):
        total = total + parts[i]
    total = jnp.where(row_iota() < 3, total, pltpu.roll(total, LANES // 2, 1))
    return lambda i: jnp.broadcast_to(total[:, i : i + 1], (ROWS, LANES))


def range_of(total):
    pick = lambda i: jnp.broadcast_to(total[:, i : i + 1], (ROWS, LANES))
    mean = pick(0) * pick(1) / jnp.maximum(pick(2) * pick(2), 1.0)
    half = 0.5 * SPAN * jnp.where(mean > 1e-6, mean, 1e-6)
    return KAPPA + half, half


def step_body(j, nblk, ghosts, last, *refs):
    refs = list(refs)
    take = lambda n: [refs.pop(0) for _ in range(n)]
    cols, table = take(1)[0], Table(take(Table.NUMBER))
    image_refs = take(6)
    basis = take(j)
    coef, gram_in, fwd_ref, bwd_ref, shear_ref, lam_ref = take(6)
    v_ref, g_ref, gram_ref = take(3)
    if not last:
        messages = take(5)
    split_ref = take(1)[0]
    f_ref, lo_ref, hi_ref = take(3)
    q_ref = None if last else take(1)[0]
    pool_n = nblk + 2 * ghosts
    centre, half = range_of(coef[...])
    inverse = (1.0 if j == 1 else 2.0) / half
    gather_image(nblk, ghosts, table, *image_refs, f_ref, lo_ref, hi_ref)
    dots = [jnp.zeros((ROWS, LANES), F32) for _ in range(j + 1)]
    for q in range(pool_n):
        prev = basis[j - 1][q]
        w = alive_of(table, q, nblk, ghosts) * f_ref[q] + KAPPA * prev
        v = (w - centre * prev) * inverse
        if j > 1:
            v = v - basis[j - 2][q]
        v_ref[q] = v
        split_ref[q] = split3(v)
        if q < nblk:
            for i in range(j):
                dots[i] = dots[i] + basis[i][q] * v
            dots[j] = dots[j] + v * v
    gram = gram_in[...]
    for i, lane in enumerate(pairs(j)):
        gram = put_dot(gram, lane, dots[i])
    energy = grads_and_spread(
        nblk, cols, fwd_ref, bwd_ref, [split_ref], shear_ref, lam_ref, [g_ref], q_ref, last
    )
    if last:
        gram_ref[...] = pack_gram(put_dot(gram, NGRAM, energy))
    else:
        finish(nblk, ghosts, table, q_ref, *messages)
        gram_ref[...] = gram


def coefficients(devices, parts, coef):
    pick = unpack_gram(devices, parts)
    g = {(i, j): pick(entry(i, j)) for i in range(ITERS) for j in range(ITERS)}
    centre, half = range_of(coef[...])

    def image(p):
        out = [None] * (len(p) + 1)

        def add(i, x):
            out[i] = x if out[i] is None else out[i] + x

        for j, x in enumerate(p):
            add(j, centre * x)
            if j == 0:
                add(1, half * x)
            else:
                add(j + 1, 0.5 * half * x)
                add(j - 1, 0.5 * half * x)
        return out

    def times(table, x, i):
        out = None
        for j, y in enumerate(x):
            term = table[i, j] * y
            out = term if out is None else out + term
        return out

    def form(x, table, y):
        out = None
        for i, z in enumerate(x):
            term = z * times(table, y, i)
            out = term if out is None else out + term
        return out

    last = ITERS - 1
    energy = {}
    for j in range(last):
        for i in range(j, ITERS):
            value = centre * g[i, j]
            if j == 0:
                value = value + half * g[i, 1]
            else:
                value = value + 0.5 * half * (g[i, j + 1] + g[i, j - 1])
            energy[i, j] = energy[j, i] = value
    energy[last, last] = pick(NGRAM) + KAPPA * g[last, last]
    one = jnp.ones((ROWS, LANES), F32)
    r, p = [one], [one]
    rr = g[0, 0]
    u = None
    for sweep in range(ITERS):
        alpha = rr / form(p, energy, p)
        if u is None:
            u = [alpha * x for x in p]
        else:
            u = [(u[i] + alpha * x) if i < len(u) else alpha * x for i, x in enumerate(p)]
        if sweep < last:
            moved = image(p)
            r = [(r[i] - alpha * x) if i < len(r) else -(alpha * x) for i, x in enumerate(moved)]
            new = form(r, g, r)
            beta = new / rr
            p = [(x + beta * p[i]) if i < len(p) else x for i, x in enumerate(r)]
            rr = new
    work = dict(g)
    lower, pivots = {}, []
    for j in range(ITERS):
        pivots.append(work[j, j])
        scale = 1.0 / work[j, j]
        for a in range(j + 1, ITERS):
            lower[a, j] = work[a, j] * scale
            for b in range(j + 1, a + 1):
                work[a, b] = work[a, b] - lower[a, j] * work[b, j]
    spread, good = None, None
    for k in range(ITERS):
        good = (pivots[k] > 0.0) if good is None else good & (pivots[k] > 0.0)
        column = {k: one}
        for i in range(k, ITERS):
            if i > k:
                column[i] = -sum(lower[i, m] * column[m] for m in range(k, i))
            term = g[k, k] * column[i] * column[i] / pivots[i]
            spread = term if spread is None else spread + term
    worst = jnp.where(good & (spread < CONDITION), 1.0, 0.0)
    live = row_iota() < 6
    return [jnp.where(live, x, 0.0) for x in u], worst


def mix(weights, refs, q):
    total = weights[0] * refs[0][q]
    for w, ref in zip(weights[1:], refs[1:]):
        total = total + w * ref[q]
    return total


def middle_body(nblk, ghosts, devices, *refs):
    refs = list(refs)
    take = lambda n: [refs.pop(0) for _ in range(n)]
    cols, table = take(1)[0], Table(take(Table.NUMBER))
    parts, coef = take(2)
    basis, grads = take(ITERS), take(ITERS)
    t_ref, gt_ref, fwd_ref, bwd_ref, shear_ref, lam_ref = take(6)
    disp_ref, gu_ref, v_ref, g_ref, gram_ref, worst_ref = take(6)
    messages, q_ref = take(5), take(1)[0]
    u, worst = coefficients(devices, parts, coef)
    worst_ref[...] = worst
    total = jnp.zeros((ROWS, LANES), F32)
    for q in range(nblk + 2 * ghosts):
        x = mix(u, basis, q)
        v = x - t_ref[q]
        v_ref[q] = v
        if q < nblk:
            for c in range(2):
                for e in range(3):
                    disp_ref[e, c : c + 1, q * LANES : (q + 1) * LANES] = x[3 * c + e : 3 * c + e + 1, :]
            total = total + v * v
    gram_ref[...] = put_dot(jnp.zeros((ROWS, LANES), F32), 0, total)
    masks = component_masks()
    q_ref[...] = jnp.zeros_like(q_ref)
    wide = [jnp.concatenate([x] * 3, axis=1) for x in u]

    def step(b, acc):
        full = mix(wide, grads, b)
        gu_ref[b] = full
        full = full - gt_ref[b]
        g_ref[b] = full
        g = [full[:, d * LANES : (d + 1) * LANES] for d in range(3)]
        stress = stress_of(g, shear_ref[b], lam_ref[b], masks)
        backward_block(b, cols, stress, bwd_ref, q_ref)
        return acc

    lax.fori_loop(0, nblk, step, 0)
    finish(nblk, ghosts, table, q_ref, *messages)


def final_body(nblk, devices, *refs):
    refs = list(refs)
    take = lambda n: [refs.pop(0) for _ in range(n)]
    parts, coef = take(2)
    grads = take(ITERS)
    gu_ref, weight_ref, worst_in, out_ref = take(4)
    u, worst = coefficients(devices, parts, coef)
    worst = jnp.minimum(worst, worst_in[...])
    row = row_iota()
    worst = jnp.where(row < 6, worst, 1.0)
    masks = component_masks()
    wide = [jnp.concatenate([x] * 3, axis=1) for x in u]
    for b in range(nblk):
        full = mix(wide, grads, b)
        a = [full[:, d * LANES : (d + 1) * LANES] for d in range(3)]
        full = gu_ref[b]
        f = [full[:, d * LANES : (d + 1) * LANES] for d in range(3)]
        traces = masks[0] * (trace_at(a, 0) * trace_at(f, 0))
        sa, sf = symmetric(a, masks), symmetric(f, masks)
        work = sa[0] * sf[0] + (sa[1] * sf[1] + sa[2] * sf[2])
        work = (masks[0] + masks[1] + masks[2]) * work
        w = weight_ref[b]
        out_ref[b : b + 1, :] = -w[:1] * jnp.sum(traces, axis=0, keepdims=True)
        out_ref[nblk + b : nblk + b + 1, :] = (-0.5 * w[:1]) * jnp.sum(work, axis=0, keepdims=True)
    out_ref[2 * nblk : 2 * nblk + ROWS, :] = worst


def closing_body(nblk, mine, other, lambda_ref, mu_ref, plain_ref):
    for b in range(nblk):
        at = slice(b * LANES, (b + 1) * LANES)
        for row, ref in ((b, lambda_ref), (nblk + b, mu_ref)):
            ref[at] = (mine[row : row + 1, :] + other[row : row + 1, :]).reshape(LANES)
    good = jnp.minimum(mine[2 * nblk :, :], other[2 * nblk :, :])
    plain_ref[0] = jnp.where(jnp.min(good) > 0.5, 0, 1)


def pairs_of(step, offset, size):
    out = []
    for t in range(size):
        u = t - offset
        if u >= 0 and u % (2 * step) < step and t + step < size:
            out += [(t, t + step), (t + step, t)]
    return out


def everywhere(x, size):
    return lax.all_to_all(jnp.broadcast_to(x[None], (size,) + x.shape), "tile", 0, 0)


HIGH = lax.Precision.HIGHEST


def extended(shard, sides, width):
    for axis, dim in sides:
        size, length = (lax.axis_size(axis), shard.shape[dim])
        up = [(i, (i + 1) % size) for i in range(size - 1)]
        down = [(j, i) for i, j in up]
        last = lax.slice_in_dim(shard, length - width, length, axis=dim)
        leading = lax.slice_in_dim(shard, 0, width, axis=dim)
        before = lax.ppermute(last, axis, up)
        after = lax.ppermute(leading, axis, down)
        shard = jnp.concatenate([before, shard, after], axis=dim)
    return shard


def plain(load, target, lame_lambda, lame_mu, volume, smooth, columns, send_list, counts):
    cases = load.shape[0]
    nblk = smooth.shape[0]
    ghosts = send_list.shape[2]
    width = smooth.shape[3]
    pool_n = nblk + 2 * ghosts
    field_shape = (cases, 3, nblk, width)
    alive = (
        (jnp.arange(nblk * width, dtype=jnp.int32) < counts[0])
        .astype(jnp.float32)
        .reshape(nblk, width)
    )
    weight = volume.reshape(nblk, width) * alive
    lam_weight = weight * lame_lambda.reshape(nblk, width)
    shear_weight = weight * lame_mu.reshape(nblk, width)
    column_hot = (columns[:, :, None] == jnp.arange(pool_n, dtype=jnp.int32)[None, None, :]).astype(
        jnp.float32
    )
    block_range = jnp.arange(nblk, dtype=jnp.int32)
    identity = jnp.eye(3, dtype=jnp.float32)
    neighbors = extended(send_list, (("tile", 0),), 1)
    below_ids = neighbors[0, 1]
    above_ids = neighbors[2, 0]
    below_hot = (below_ids[:, None] == block_range[None, :]).astype(jnp.float32)
    above_hot = (above_ids[:, None] == block_range[None, :]).astype(jnp.float32)

    def collect(field):
        padded = extended(field, (("tile", 2),), nblk)
        from_left = jnp.take(padded[:, :, :nblk], below_ids, axis=2)
        from_right = jnp.take(padded[:, :, 2 * nblk :], above_ids, axis=2)
        return jnp.concatenate([field, from_left, from_right], axis=2)

    def send_back(lower_part, upper_part):
        to_lower = jnp.einsum("cegj,gb->cebj", lower_part, below_hot, precision=HIGH)
        to_upper = jnp.einsum("cegj,gb->cebj", upper_part, above_hot, precision=HIGH)
        padded = extended(jnp.concatenate([to_lower, to_upper], axis=2), (("tile", 2),), nblk)
        return padded[:, :, :nblk] + padded[:, :, 3 * nblk :]

    def strains(field):
        pooled = collect(field * alive)
        gathered = jnp.einsum("ceqj,bkq->cebkj", pooled, column_hot, precision=HIGH)
        return jnp.einsum("bkdij,cebkj->cedbi", smooth, gathered, precision=HIGH)

    def operate(field):
        grads = strains(field)
        trace_u = grads[:, 0, 0] + grads[:, 1, 1] + grads[:, 2, 2]
        strain = 0.5 * (grads + jnp.swapaxes(grads, 1, 2))
        stress = (
            2.0 * shear_weight * strain
            + (lam_weight * trace_u)[:, None, None] * identity[None, :, :, None, None]
        )
        contrib = jnp.einsum("bkdij,cedbi->cebkj", smooth, stress, precision=HIGH)
        pooled = jnp.einsum("cebkj,bkq->ceqj", contrib, column_hot, precision=HIGH)
        own = pooled[:, :, :nblk]
        returned = send_back(pooled[:, :, nblk : nblk + ghosts], pooled[:, :, nblk + ghosts :])
        return alive * (own + returned) + KAPPA * field

    def curvature(first, second):
        return over_tiles(jnp.sum(first * second, axis=(1, 2, 3)))

    def squares(residual):
        return over_tiles(jnp.sum(residual * residual, axis=(1, 2, 3)))

    def over_tiles(x):
        size = lax.axis_size("tile")
        block = jnp.zeros((ROWS, LANES), F32).at[0, :cases].set(x)
        return jnp.sum(everywhere(block, size), axis=0)[0, :cases]

    def widen(scalars):
        return scalars[:, None, None, None]

    def run_solver(rhs):
        def sweep(i, state):
            solution, residual, direction, norm_now = state
            image = operate(direction)
            step_len = norm_now / curvature(direction, image)
            solution = solution + widen(step_len) * direction
            residual = residual - widen(step_len) * image
            norm_next = squares(residual)
            direction = residual + widen(norm_next / norm_now) * direction
            return solution, residual, direction, norm_next

        start = (jnp.zeros_like(rhs), rhs, rhs, squares(rhs))
        return lax.fori_loop(0, ITERS, sweep, start)[0]

    def phase(i, state):
        _, forward = state
        first = alive * load.reshape(field_shape)
        second = alive * (forward - target.reshape(field_shape))
        return forward, run_solver(jnp.where(i == 0, first, second))

    blank = jnp.zeros(field_shape, F32)
    forward, adjoint = lax.fori_loop(0, 2, phase, (blank, blank))
    grads = strains(jnp.concatenate([forward, adjoint], axis=0))
    grads_u = grads[:cases]
    grads_a = grads[cases:]
    trace_u = grads_u[:, 0, 0] + grads_u[:, 1, 1] + grads_u[:, 2, 2]
    trace_a = grads_a[:, 0, 0] + grads_a[:, 1, 1] + grads_a[:, 2, 2]
    strain_u = 0.5 * (grads_u + jnp.swapaxes(grads_u, 1, 2))
    strain_a = 0.5 * (grads_a + jnp.swapaxes(grads_a, 1, 2))
    local_lambda = (-weight * jnp.sum(trace_u * trace_a, axis=0)).reshape(-1)
    local_mu = (-2.0 * weight * jnp.sum(strain_u * strain_a, axis=(0, 1, 2))).reshape(-1)
    local = jnp.stack([local_lambda, local_mu])
    grad_lambda, grad_mu = local + lax.ppermute(local, "case", [(0, 1), (1, 0)])
    return (forward.reshape(load.shape), grad_lambda, grad_mu)


def shards(load, target, lame_lambda, lame_mu, volume, smooth, columns, send_list, counts):
    cases = load.shape[0]
    nblk = smooth.shape[0]
    ghosts = send_list.shape[2]
    pool_n = nblk + 2 * ghosts
    tiles, size = lax.axis_size("tile"), load.shape[2]
    place = lax.axis_index("tile").astype(jnp.int32).reshape(1)
    block = lambda n: arr(n, ROWS, LANES)
    wide = lambda n: arr(n, ROWS, 3 * LANES)
    tile8 = arr(ROWS, LANES)
    v_own, t_own, up, down, lam, shear, weight, mask, coef = call(
        functools.partial(prepare_body, nblk, ghosts),
        [block(nblk)] * 2 + [block(2 * ghosts + 1)] * 2 + [block(nblk)] * 3 + [tile8] * 2,
        [SM] * 3 + [pl.BlockSpec(memory_space=pltpu.HBM)] * 6,
        [pltpu.VMEM(x, F32) for x in ((3, cases, size), (3, cases, size), (size,), (size,), (size,), (2, 3, LANES, LANES))]
        + [pltpu.SemaphoreType.DMA((6,))],
    )(
        place, send_list, counts, in_hbm(load.transpose(1, 0, 2)), in_hbm(target.transpose(1, 0, 2)),
        in_hbm(lame_lambda), in_hbm(lame_mu), in_hbm(volume), in_hbm(smooth),
    )
    below = lax.ppermute(up, "tile", [(t, t + 1) for t in range(tiles - 1)])
    above = lax.ppermute(down, "tile", [(t + 1, t) for t in range(tiles - 1)])
    hops, step = [coef], 1
    while step < tiles:
        hops.append(hops[-1] + lax.ppermute(hops[-1], "tile", pairs_of(step, 0, tiles)))
        step *= 2
    coef = hops[-1]
    fwd, bwd = convert(smooth, hops[1])
    numbers = lambda x: x[2 * ghosts, 0, : Table.SIZE].astype(jnp.int32)
    table = (place, send_list, counts, numbers(below), numbers(above))
    matrix_scratch = pltpu.VMEM((pool_n, 3 * ROWS, LANES), BF16)
    pool_scratch = pltpu.VMEM((pool_n, ROWS, LANES), F32)
    side_scratch = pltpu.VMEM((nblk, ROWS, LANES), F32)
    msgs = [block(nblk)] + [block(2 * ghosts)] * 4
    scalars = [SM] * Table.NUMBER
    v0, t_pool, g0, gt, *rest, gram = call(
        functools.partial(first_body, nblk, ghosts),
        [block(pool_n)] * 2 + [wide(nblk)] * 2 + msgs + [tile8],
        [SM] + scalars + [VM] * 9,
        [matrix_scratch, matrix_scratch, pool_scratch],
    )(columns, *table, v_own, t_own, below, above, fwd, bwd, shear, lam, hops[min(2, len(hops) - 1)])

    def exchange(own, near, first, second, ghost, mask=mask):
        near = lax.ppermute(near, "tile", pairs_of(1, 0, tiles))
        first = lax.ppermute(first, "tile", pairs_of(2, 0, tiles))
        second = lax.ppermute(second, "tile", pairs_of(2, 2, tiles))
        relay = lax.ppermute(jnp.where(mask[None] > 0.0, first, second), "tile", pairs_of(1, 0, tiles))
        return own, ghost, near, relay, first, second

    def advance(j, basis, gram, rest):
        final = j == ITERS - 1
        ins = list(exchange(*rest))
        ins += list(basis) + [coef, gram, fwd, bwd, shear, lam]
        scratch = [matrix_scratch, pool_scratch, side_scratch, side_scratch]
        if not final:
            scratch.append(pool_scratch)
        return call(
            functools.partial(step_body, j, nblk, ghosts, final),
            [block(pool_n), wide(nblk)] + ([tile8] if final else [tile8] + msgs),
            [SM] + scalars + [VM] * len(ins),
            scratch,
        )(columns, *table, *ins)

    basis, grads = [v0], [g0]
    for j in range(1, ITERS):
        v, g, gram, *rest = advance(j, basis, gram, rest)
        basis.append(v)
        grads.append(g)
    disp, gu, v0, g0, gram, worst, *rest = call(
        functools.partial(middle_body, nblk, ghosts, tiles),
        [arr(3, cases, size), wide(nblk), block(pool_n), wide(nblk), tile8, tile8] + msgs,
        [SM] + scalars + [VM] * (2 + 2 * ITERS + 6),
        [pool_scratch],
    )(columns, *table, everywhere(gram, tiles), coef, *basis, *grads, t_pool, gt, fwd, bwd, shear, lam)
    basis, grads = [v0], [g0]
    for j in range(1, ITERS):
        v, g, gram, *rest = advance(j, basis, gram, rest)
        basis.append(v)
        grads.append(g)
    out = call(
        functools.partial(final_body, nblk, tiles),
        [arr(2 * nblk + ROWS, LANES)],
        [VM] * (2 + ITERS + 3),
    )(everywhere(gram, tiles), coef, *grads, gu, weight, worst)[0]
    other = lax.ppermute(out, "case", [(0, 1), (1, 0)])
    grad_lambda, grad_mu, again = pl.pallas_call(
        functools.partial(closing_body, nblk),
        out_shape=[arr(size), arr(size), arr(1, dtype=jnp.int32)],
        in_specs=[VM, VM],
        out_specs=[VM, VM, SM],
        compiler_params=pltpu.CompilerParams(vmem_limit_bytes=LIMIT),
    )(out, other)
    return lax.cond(
        again[0] > 0,
        lambda: plain(load, target, lame_lambda, lame_mu, volume, smooth, columns, send_list, counts),
        lambda: (disp.transpose(1, 0, 2), grad_lambda, grad_mu),
    )


def solution(mesh):
    return jax.shard_map(
        shards,
        mesh=mesh,
        in_specs=(
            P("case", None, "tile"),
            P("case", None, "tile"),
            P("tile"),
            P("tile"),
            P("tile"),
            P("tile", None, None, None, None),
            P("tile", None),
            P("tile", None, None),
            P("tile"),
        ),
        out_specs=(P("case", None, "tile"), P("tile"), P("tile")),
        check_vma=False,
    )
```

```python
import functools

import jax
import jax.numpy as jnp
from jax import lax
from jax.experimental import pallas as pl
from jax.experimental.pallas import tpu as pltpu
from jax.sharding import PartitionSpec as P

ITERS = 6
KAPPA = 0.5
CONDITION = 4000.0
SPAN = 7.2
ROWS = 8
LANES = 128
F32 = jnp.float32
BF16 = jnp.bfloat16
LIMIT = 14 * 1024 * 1024

VM = pl.BlockSpec(memory_space=pltpu.VMEM)
SM = pl.BlockSpec(memory_space=pltpu.SMEM)


def call(body, outs, ins, scratch=(), flops=0, nbytes=0, limit=LIMIT):
    return pl.pallas_call(
        body,
        out_shape=outs,
        in_specs=ins,
        out_specs=jax.tree.map(lambda _: VM, outs),
        scratch_shapes=list(scratch),
        compiler_params=pltpu.CompilerParams(vmem_limit_bytes=limit),
        cost_estimate=pl.CostEstimate(flops=flops, bytes_accessed=nbytes, transcendentals=0),
    )


def arr(*shape, dtype=F32):
    return jax.ShapeDtypeStruct(shape, dtype)


def in_hbm(x):
    return pltpu.with_memory_space_constraint(x, pltpu.HBM)


def lane_iota():
    return lax.broadcasted_iota(jnp.int32, (ROWS, LANES), 1)


def row_iota():
    return lax.broadcasted_iota(jnp.int32, (ROWS, LANES), 0)


def split3(x):
    hi = x.astype(BF16)
    rest = x - hi.astype(F32)
    mid = rest.astype(BF16)
    low = (rest - mid.astype(F32)).astype(BF16)
    return jnp.concatenate([hi, mid, low], axis=0)


def fold3(y):
    return y[:ROWS] + (y[ROWS : 2 * ROWS] + y[2 * ROWS : 3 * ROWS])


def component_masks():
    row = row_iota()
    comp = lax.rem(row, 3)
    live = row < 6
    return [(live & (comp == e)).astype(F32) for e in range(3)]


def shift_rows(x, by):
    by = by % ROWS
    return x if by == 0 else pltpu.roll(x, by, 0)


def symmetric(g, masks):
    out = []
    for d in range(3):
        total = g[d]
        for e in range(3):
            total = total + masks[e] * shift_rows(g[e], e - d)
        out.append(total)
    return out


def trace_at(g, d):
    return shift_rows(g[0], d) + shift_rows(g[1], d - 1) + shift_rows(g[2], d - 2)


def stress_of(g, shear, lam, masks):
    sym = symmetric(g, masks)
    return [shear * sym[d] + lam * (masks[d] * trace_at(g, d)) for d in range(3)]


def forward_block(b, cols, split_refs, fwd_ref):
    sides = []
    for ref in split_refs:
        line = jnp.concatenate([ref[cols[b, k]] for k in range(4)], axis=1)
        sides.append(line)
    line = sides[0] if len(sides) == 1 else jnp.concatenate(sides, axis=0)
    out = jnp.dot(
        jnp.concatenate([line, line], axis=1), fwd_ref[b], preferred_element_type=F32
    )
    return [fold3(out[3 * ROWS * i : 3 * ROWS * (i + 1)]) for i in range(len(sides))]


def backward_block(b, cols, stress, bwd_ref, q_ref):
    parts = split3(jnp.concatenate(stress, axis=1))
    out = jnp.dot(
        jnp.concatenate([parts, parts], axis=1), bwd_ref[b], preferred_element_type=F32
    )
    out = fold3(out)
    for k in range(4):
        q = cols[b, k]
        q_ref[q] = q_ref[q] + out[:, k * LANES : (k + 1) * LANES]


def put_dot(acc, lane, x):
    total = jnp.sum(x, axis=1, keepdims=True)
    return jnp.where(lane_iota() == lane, total, acc)


def over_components(x, masks):
    total = None
    for shift in (-2, -1, 0, 1, 2):
        moved = shift_rows(x, shift)
        for e in range(3):
            if 0 <= e - shift < 3:
                term = masks[e] * moved
                total = term if total is None else total + term
    return total


def pairs(j):
    return [j * (j + 1) // 2 + i for i in range(j + 1)]


def entry(i, j):
    i, j = min(i, j), max(i, j)
    return j * (j + 1) // 2 + i


NGRAM = ITERS * (ITERS + 1) // 2


class Table:
    NUMBER = 5
    UP, DOWN, COUNT, SIZE = 0, 8, 16, 17

    def __init__(self, refs):
        self.place, self.sends, self.counts, self.below, self.above = refs
        self.core = lax.rem(self.place[0], 2)
        self.even = lax.rem(self.place[0], 4) < 2

    def up(self, g):
        return self.sends[0, 1, g]

    def down(self, g):
        return self.sends[0, 0, g]


def alive_of(table, q, nblk, ghosts):
    if q < nblk:
        start, count = q * LANES, table.counts[0]
    elif q < nblk + ghosts:
        start, count = table.below[Table.UP + q - nblk] * LANES, table.below[Table.COUNT]
    else:
        start, count = table.above[Table.DOWN + q - nblk - ghosts] * LANES, table.above[Table.COUNT]
    return (lane_iota() + start < count).astype(F32)


DEPTH = 4


def convert_body(nblk, s_hbm, after, fwd_ref, bwd_ref, buf, sem):
    def copy(b, slot):
        return pltpu.make_async_copy(s_hbm.at[b], buf.at[slot], sem.at[slot])

    for b in range(min(DEPTH, nblk)):
        copy(b, b).start()

    def step(b, carry):
        slot = lax.rem(b, DEPTH)
        copy(b, slot).wait()
        for k in range(4):
            for d in range(3):
                x = buf[slot, k, d]
                rows, lanes = slice(d * LANES, (d + 1) * LANES), slice(k * LANES, (k + 1) * LANES)
                for y, ref, first, second, size in (
                    (x, bwd_ref, rows, lanes, 3 * LANES),
                    (x.T, fwd_ref, lanes, rows, 4 * LANES),
                ):
                    hi = y.astype(BF16)
                    ref[b, first, second] = hi
                    ref[b, slice(first.start + size, first.stop + size), second] = (
                        y - hi.astype(F32)
                    ).astype(BF16)

        @pl.when(b + DEPTH < nblk)
        def _():
            copy(b + DEPTH, slot).start()

        return carry

    lax.fori_loop(0, nblk, step, 0)


def convert(smooth, after):
    nblk = smooth.shape[0]
    return call(
        functools.partial(convert_body, nblk),
        [
            arr(nblk, 8 * LANES, 3 * LANES, dtype=BF16),
            arr(nblk, 6 * LANES, 4 * LANES, dtype=BF16),
        ],
        [pl.BlockSpec(memory_space=pltpu.HBM), VM],
        [pltpu.VMEM((DEPTH,) + smooth.shape[1:], F32), pltpu.SemaphoreType.DMA((DEPTH,))],
        flops=smooth.size * 3,
        nbytes=smooth.size * 12,
    )(in_hbm(smooth), after)


def prepare_body(nblk, ghosts, place, sends, counts, *refs):
    sources, outs, scratch, sem = refs[:6], refs[6:15], refs[15:21], refs[21]
    nrows = nblk * LANES
    copies = [pltpu.make_async_copy(x, y, sem.at[i]) for i, (x, y) in enumerate(zip((*sources[:5], sources[5].at[0, :1]), scratch))]
    for copy in copies:
        copy.start()
    for copy in copies:
        copy.wait()
    load, target, lam, mu, volume, piece = scratch
    v_ref, t_ref, up_ref, down_ref, lam_ref, shear_ref, weight_ref, mask_ref, sample_ref = outs
    row, lane = row_iota(), lane_iota()
    zero = jnp.zeros((ROWS, LANES), F32)
    for b in range(nblk):
        at = slice(b * LANES, (b + 1) * LANES)
        alive = (lane + b * LANES < counts[0]).astype(F32)
        for src, dst in ((load, v_ref), (target, t_ref)):
            x = zero
            for c in range(2):
                for e in range(3):
                    x = jnp.where(row == 3 * c + e, src[e, c : c + 1, at], x)
            dst[b] = x * alive
        tall = lambda x: jnp.broadcast_to(x[at].reshape(1, LANES), (ROWS, LANES))
        weight = tall(volume) * alive
        weight_ref[b] = weight
        lam_ref[b] = weight * tall(lam)
        shear_ref[b] = weight * tall(mu)
    meta = jnp.where(lane == Table.COUNT, counts[0].astype(F32), zero)
    for g in range(ghosts):
        meta = jnp.where(lane == Table.UP + g, sends[0, 1, g].astype(F32), meta)
        meta = jnp.where(lane == Table.DOWN + g, sends[0, 0, g].astype(F32), meta)
    for side, ref in ((1, up_ref), (0, down_ref)):
        for g in range(ghosts):
            ref[g] = v_ref[sends[0, side, g]]
            ref[ghosts + g] = t_ref[sends[0, side, g]]
        ref[2 * ghosts] = meta
    forward_first = (lax.rem(place[0], 4) < 2) == (lax.rem(place[0], 2) == 0)
    mask_ref[...] = jnp.where(forward_first, 1.0, zero)
    square = piece[0, 0] * piece[0, 0]
    for d in range(1, 3):
        square = square + piece[0, d] * piece[0, d]
    factor = 4.0 * shear_ref[0] + lam_ref[0]
    total = jnp.dot(factor, square, preferred_element_type=F32)
    total = jnp.sum(total, axis=1, keepdims=True) * (4.0 / (3 * LANES))
    share = counts[0].astype(F32) * (1.0 / nrows)
    sample_ref[...] = jnp.where(lane == 0, total, jnp.where(lane == 1, share, jnp.where(lane == 2, 1.0, 0.0)))


def split_pool(v_ref, split_ref, pool_n):
    for q in range(pool_n):
        split_ref[q] = split3(v_ref[q])


def finish(nblk, ghosts, table, q_ref, own_ref, near_ref, first_ref, second_ref, ghost_ref):
    own_ref[...] = q_ref[:nblk]
    ghost_ref[...] = q_ref[nblk:]
    for g in range(2 * ghosts):
        if g < ghosts:
            up, down = q_ref[nblk + ghosts + g], q_ref[nblk + g]
        else:
            up, down = q_ref[table.up(g - ghosts)], q_ref[table.down(g - ghosts)]
        near_ref[g] = jnp.where(table.core == 0, up, down)
        first_ref[g] = jnp.where(table.even, up, down)
        second_ref[g] = jnp.where(table.even, down, up)


def grads_and_spread(nblk, cols, fwd_ref, bwd_ref, split_refs, shear_ref, lam_ref, g_refs, q_ref, energy):
    masks = component_masks()
    if q_ref is not None:
        q_ref[...] = jnp.zeros_like(q_ref)

    def use(b, full, acc):
        for ref, x in zip(g_refs, full):
            ref[b] = x
        if not energy and q_ref is None:
            return acc
        g = [full[0][:, d * LANES : (d + 1) * LANES] for d in range(3)]
        stress = stress_of(g, shear_ref[b], lam_ref[b], masks)
        if energy:
            acc = acc + (stress[0] * g[0] + (stress[1] * g[1] + stress[2] * g[2]))
        if q_ref is not None:
            backward_block(b, cols, stress, bwd_ref, q_ref)
        return acc

    def forward(b):
        return forward_block(b, cols, split_refs, fwd_ref)

    def step(i, carry):
        full, acc = carry
        after = forward(2 * i + 1)
        acc = use(2 * i, full, acc)
        full = forward(jnp.minimum(2 * i + 2, nblk - 1))
        acc = use(2 * i + 1, after, acc)
        return full, acc

    start = (forward(0), jnp.zeros((ROWS, LANES), F32))
    full, acc = lax.fori_loop(0, nblk // 2, step, start, unroll=2 if energy and nblk % 4 == 0 else 1)
    if nblk % 2:
        acc = use(nblk - 1, full, acc)
    return acc


def first_body(nblk, ghosts, cols, *refs):
    table = Table(refs[: Table.NUMBER])
    v_own, t_own, below, above, fwd_ref, bwd_ref, shear_ref, lam_ref, _ = refs[Table.NUMBER : Table.NUMBER + 9]
    refs = refs[Table.NUMBER + 9 :]
    v_ref, t_ref, g_ref, gt_ref = refs[:4]
    messages, gram_ref, (split_ref, split_t, q_ref) = refs[4:9], refs[9], refs[10:]
    pool_n = nblk + 2 * ghosts
    v_ref[:nblk] = v_own[...]
    t_ref[:nblk] = t_own[...]
    for g in range(ghosts):
        v_ref[nblk + g] = below[g]
        t_ref[nblk + g] = below[ghosts + g]
        v_ref[nblk + ghosts + g] = above[g]
        t_ref[nblk + ghosts + g] = above[ghosts + g]
    split_pool(v_ref, split_ref, pool_n)
    split_pool(t_ref, split_t, pool_n)
    grads_and_spread(
        nblk, cols, fwd_ref, bwd_ref, [split_ref, split_t], shear_ref, lam_ref, [g_ref, gt_ref], q_ref, False
    )
    finish(nblk, ghosts, table, q_ref, *messages)
    total = jnp.zeros((ROWS, LANES), F32)
    for b in range(nblk):
        total = total + v_ref[b] * v_ref[b]
    gram_ref[...] = put_dot(jnp.zeros((ROWS, LANES), F32), 0, total)


def gather_image(nblk, ghosts, table, own, ghost, near, relay, first, second, f_ref, lo_ref, hi_ref):
    f_ref[:nblk] = own[...]
    lo_ref[...] = jnp.zeros_like(lo_ref)
    hi_ref[...] = jnp.zeros_like(hi_ref)
    low = table.core == 0
    below1 = lambda g: jnp.where(low, relay[g], near[g])
    above1 = lambda g: jnp.where(low, near[g], relay[g])
    below2 = lambda g: jnp.where(table.even, second[g], first[g])
    above2 = lambda g: jnp.where(table.even, first[g], second[g])

    def add(ref, at, x):
        ref[at] = ref[at] + x

    for g in range(ghosts):
        add(f_ref, table.up(g), above1(g))
        add(lo_ref, table.below[Table.UP + g], ghost[g])
        add(hi_ref, table.above[Table.DOWN + g], ghost[ghosts + g])
    for g in range(ghosts):
        add(f_ref, table.down(g), below1(g))
        add(lo_ref, table.below[Table.DOWN + g], below2(g))
        add(hi_ref, table.above[Table.UP + g], above2(g))
    for g in range(ghosts):
        f_ref[nblk + g] = below1(ghosts + g) + lo_ref[table.below[Table.UP + g]]
        f_ref[nblk + ghosts + g] = above1(ghosts + g) + hi_ref[table.above[Table.DOWN + g]]


def pack_gram(gram):
    total = over_components(gram, component_masks())
    low = lax.broadcasted_iota(jnp.int32, (1, LANES), 1) < LANES // 2
    row = jnp.where(low, total[:1], pltpu.roll(total, LANES // 2, 1)[3:4])
    return jnp.broadcast_to(row, (ROWS, LANES))


def unpack_gram(devices, parts):
    total = parts[0]
    for i in range(1, devices):
        total = total + parts[i]
    total = jnp.where(row_iota() < 3, total, pltpu.roll(total, LANES // 2, 1))
    return lambda i: jnp.broadcast_to(total[:, i : i + 1], (ROWS, LANES))


def range_of(total):
    pick = lambda i: jnp.broadcast_to(total[:, i : i + 1], (ROWS, LANES))
    mean = pick(0) * pick(1) / jnp.maximum(pick(2) * pick(2), 1.0)
    half = 0.5 * SPAN * jnp.where(mean > 1e-6, mean, 1e-6)
    return KAPPA + half, half


def step_body(j, nblk, ghosts, last, *refs):
    refs = list(refs)
    take = lambda n: [refs.pop(0) for _ in range(n)]
    cols, table = take(1)[0], Table(take(Table.NUMBER))
    image_refs = take(6)
    basis = take(j)
    coef, gram_in, fwd_ref, bwd_ref, shear_ref, lam_ref = take(6)
    v_ref, g_ref, gram_ref = take(3)
    if not last:
        messages = take(5)
    split_ref = take(1)[0]
    f_ref, lo_ref, hi_ref = take(3)
    q_ref = None if last else take(1)[0]
    pool_n = nblk + 2 * ghosts
    centre, half = range_of(coef[...])
    inverse = (1.0 if j == 1 else 2.0) / half
    gather_image(nblk, ghosts, table, *image_refs, f_ref, lo_ref, hi_ref)
    dots = [jnp.zeros((ROWS, LANES), F32) for _ in range(j + 1)]
    for q in range(pool_n):
        prev = basis[j - 1][q]
        w = alive_of(table, q, nblk, ghosts) * f_ref[q] + KAPPA * prev
        v = (w - centre * prev) * inverse
        if j > 1:
            v = v - basis[j - 2][q]
        v_ref[q] = v
        split_ref[q] = split3(v)
        if q < nblk:
            for i in range(j):
                dots[i] = dots[i] + basis[i][q] * v
            dots[j] = dots[j] + v * v
    gram = gram_in[...]
    for i, lane in enumerate(pairs(j)):
        gram = put_dot(gram, lane, dots[i])
    energy = grads_and_spread(
        nblk, cols, fwd_ref, bwd_ref, [split_ref], shear_ref, lam_ref, [g_ref], q_ref, last
    )
    if last:
        gram_ref[...] = pack_gram(put_dot(gram, NGRAM, energy))
    else:
        finish(nblk, ghosts, table, q_ref, *messages)
        gram_ref[...] = gram


def coefficients(devices, parts, coef):
    pick = unpack_gram(devices, parts)
    g = {(i, j): pick(entry(i, j)) for i in range(ITERS) for j in range(ITERS)}
    centre, half = range_of(coef[...])

    def image(p):
        out = [None] * (len(p) + 1)

        def add(i, x):
            out[i] = x if out[i] is None else out[i] + x

        for j, x in enumerate(p):
            add(j, centre * x)
            if j == 0:
                add(1, half * x)
            else:
                add(j + 1, 0.5 * half * x)
                add(j - 1, 0.5 * half * x)
        return out

    def times(table, x, i):
        out = None
        for j, y in enumerate(x):
            term = table[i, j] * y
            out = term if out is None else out + term
        return out

    def form(x, table, y):
        out = None
        for i, z in enumerate(x):
            term = z * times(table, y, i)
            out = term if out is None else out + term
        return out

    last = ITERS - 1
    energy = {}
    for j in range(last):
        for i in range(j, ITERS):
            value = centre * g[i, j]
            if j == 0:
                value = value + half * g[i, 1]
            else:
                value = value + 0.5 * half * (g[i, j + 1] + g[i, j - 1])
            energy[i, j] = energy[j, i] = value
    energy[last, last] = pick(NGRAM) + KAPPA * g[last, last]
    one = jnp.ones((ROWS, LANES), F32)
    r, p = [one], [one]
    rr = g[0, 0]
    u = None
    for sweep in range(ITERS):
        alpha = rr / form(p, energy, p)
        if u is None:
            u = [alpha * x for x in p]
        else:
            u = [(u[i] + alpha * x) if i < len(u) else alpha * x for i, x in enumerate(p)]
        if sweep < last:
            moved = image(p)
            r = [(r[i] - alpha * x) if i < len(r) else -(alpha * x) for i, x in enumerate(moved)]
            new = form(r, g, r)
            beta = new / rr
            p = [(x + beta * p[i]) if i < len(p) else x for i, x in enumerate(r)]
            rr = new
    work = dict(g)
    lower, pivots = {}, []
    for j in range(ITERS):
        pivots.append(work[j, j])
        scale = 1.0 / work[j, j]
        for a in range(j + 1, ITERS):
            lower[a, j] = work[a, j] * scale
            for b in range(j + 1, a + 1):
                work[a, b] = work[a, b] - lower[a, j] * work[b, j]
    spread, good = None, None
    for k in range(ITERS):
        good = (pivots[k] > 0.0) if good is None else good & (pivots[k] > 0.0)
        column = {k: one}
        for i in range(k, ITERS):
            if i > k:
                column[i] = -sum(lower[i, m] * column[m] for m in range(k, i))
            term = g[k, k] * column[i] * column[i] / pivots[i]
            spread = term if spread is None else spread + term
    worst = jnp.where(good & (spread < CONDITION), 1.0, 0.0)
    live = row_iota() < 6
    return [jnp.where(live, x, 0.0) for x in u], worst


def mix(weights, refs, q):
    total = weights[0] * refs[0][q]
    for w, ref in zip(weights[1:], refs[1:]):
        total = total + w * ref[q]
    return total


def middle_body(nblk, ghosts, devices, *refs):
    refs = list(refs)
    take = lambda n: [refs.pop(0) for _ in range(n)]
    cols, table = take(1)[0], Table(take(Table.NUMBER))
    parts, coef = take(2)
    basis, grads = take(ITERS), take(ITERS)
    t_ref, gt_ref, fwd_ref, bwd_ref, shear_ref, lam_ref = take(6)
    disp_ref, gu_ref, v_ref, g_ref, gram_ref, worst_ref = take(6)
    messages, q_ref = take(5), take(1)[0]
    u, worst = coefficients(devices, parts, coef)
    worst_ref[...] = worst
    total = jnp.zeros((ROWS, LANES), F32)
    for q in range(nblk + 2 * ghosts):
        x = mix(u, basis, q)
        v = x - t_ref[q]
        v_ref[q] = v
        if q < nblk:
            for c in range(2):
                for e in range(3):
                    disp_ref[e, c : c + 1, q * LANES : (q + 1) * LANES] = x[3 * c + e : 3 * c + e + 1, :]
            total = total + v * v
    gram_ref[...] = put_dot(jnp.zeros((ROWS, LANES), F32), 0, total)
    masks = component_masks()
    q_ref[...] = jnp.zeros_like(q_ref)
    wide = [jnp.concatenate([x] * 3, axis=1) for x in u]

    def step(b, acc):
        full = mix(wide, grads, b)
        gu_ref[b] = full
        full = full - gt_ref[b]
        g_ref[b] = full
        g = [full[:, d * LANES : (d + 1) * LANES] for d in range(3)]
        stress = stress_of(g, shear_ref[b], lam_ref[b], masks)
        backward_block(b, cols, stress, bwd_ref, q_ref)
        return acc

    lax.fori_loop(0, nblk, step, 0)
    finish(nblk, ghosts, table, q_ref, *messages)


def final_body(nblk, devices, *refs):
    refs = list(refs)
    take = lambda n: [refs.pop(0) for _ in range(n)]
    parts, coef = take(2)
    grads = take(ITERS)
    gu_ref, weight_ref, worst_in, out_ref = take(4)
    u, worst = coefficients(devices, parts, coef)
    worst = jnp.minimum(worst, worst_in[...])
    row = row_iota()
    worst = jnp.where(row < 6, worst, 1.0)
    masks = component_masks()
    wide = [jnp.concatenate([x] * 3, axis=1) for x in u]
    for b in range(nblk):
        full = mix(wide, grads, b)
        a = [full[:, d * LANES : (d + 1) * LANES] for d in range(3)]
        full = gu_ref[b]
        f = [full[:, d * LANES : (d + 1) * LANES] for d in range(3)]
        traces = masks[0] * (trace_at(a, 0) * trace_at(f, 0))
        sa, sf = symmetric(a, masks), symmetric(f, masks)
        work = sa[0] * sf[0] + (sa[1] * sf[1] + sa[2] * sf[2])
        work = (masks[0] + masks[1] + masks[2]) * work
        w = weight_ref[b]
        out_ref[b : b + 1, :] = -w[:1] * jnp.sum(traces, axis=0, keepdims=True)
        out_ref[nblk + b : nblk + b + 1, :] = (-0.5 * w[:1]) * jnp.sum(work, axis=0, keepdims=True)
    out_ref[2 * nblk : 2 * nblk + ROWS, :] = worst


def closing_body(nblk, mine, other, lambda_ref, mu_ref, plain_ref):
    for b in range(nblk):
        at = slice(b * LANES, (b + 1) * LANES)
        for row, ref in ((b, lambda_ref), (nblk + b, mu_ref)):
            ref[at] = (mine[row : row + 1, :] + other[row : row + 1, :]).reshape(LANES)
    good = jnp.minimum(mine[2 * nblk :, :], other[2 * nblk :, :])
    plain_ref[0] = jnp.where(jnp.min(good) > 0.5, 0, 1)


def pairs_of(step, offset, size):
    out = []
    for t in range(size):
        u = t - offset
        if u >= 0 and u % (2 * step) < step and t + step < size:
            out += [(t, t + step), (t + step, t)]
    return out


def everywhere(x, size):
    return lax.all_to_all(jnp.broadcast_to(x[None], (size,) + x.shape), "tile", 0, 0)


HIGH = lax.Precision.HIGHEST


def extended(shard, sides, width):
    for axis, dim in sides:
        size, length = (lax.axis_size(axis), shard.shape[dim])
        up = [(i, (i + 1) % size) for i in range(size - 1)]
        down = [(j, i) for i, j in up]
        last = lax.slice_in_dim(shard, length - width, length, axis=dim)
        leading = lax.slice_in_dim(shard, 0, width, axis=dim)
        before = lax.ppermute(last, axis, up)
        after = lax.ppermute(leading, axis, down)
        shard = jnp.concatenate([before, shard, after], axis=dim)
    return shard


def plain(load, target, lame_lambda, lame_mu, volume, smooth, columns, send_list, counts):
    cases = load.shape[0]
    nblk = smooth.shape[0]
    ghosts = send_list.shape[2]
    width = smooth.shape[3]
    pool_n = nblk + 2 * ghosts
    field_shape = (cases, 3, nblk, width)
    alive = (
        (jnp.arange(nblk * width, dtype=jnp.int32) < counts[0])
        .astype(jnp.float32)
        .reshape(nblk, width)
    )
    weight = volume.reshape(nblk, width) * alive
    lam_weight = weight * lame_lambda.reshape(nblk, width)
    shear_weight = weight * lame_mu.reshape(nblk, width)
    column_hot = (columns[:, :, None] == jnp.arange(pool_n, dtype=jnp.int32)[None, None, :]).astype(
        jnp.float32
    )
    block_range = jnp.arange(nblk, dtype=jnp.int32)
    identity = jnp.eye(3, dtype=jnp.float32)
    neighbors = extended(send_list, (("tile", 0),), 1)
    below_ids = neighbors[0, 1]
    above_ids = neighbors[2, 0]
    below_hot = (below_ids[:, None] == block_range[None, :]).astype(jnp.float32)
    above_hot = (above_ids[:, None] == block_range[None, :]).astype(jnp.float32)

    def collect(field):
        padded = extended(field, (("tile", 2),), nblk)
        from_left = jnp.take(padded[:, :, :nblk], below_ids, axis=2)
        from_right = jnp.take(padded[:, :, 2 * nblk :], above_ids, axis=2)
        return jnp.concatenate([field, from_left, from_right], axis=2)

    def send_back(lower_part, upper_part):
        to_lower = jnp.einsum("cegj,gb->cebj", lower_part, below_hot, precision=HIGH)
        to_upper = jnp.einsum("cegj,gb->cebj", upper_part, above_hot, precision=HIGH)
        padded = extended(jnp.concatenate([to_lower, to_upper], axis=2), (("tile", 2),), nblk)
        return padded[:, :, :nblk] + padded[:, :, 3 * nblk :]

    def strains(field):
        pooled = collect(field * alive)
        gathered = jnp.einsum("ceqj,bkq->cebkj", pooled, column_hot, precision=HIGH)
        return jnp.einsum("bkdij,cebkj->cedbi", smooth, gathered, precision=HIGH)

    def operate(field):
        grads = strains(field)
        trace_u = grads[:, 0, 0] + grads[:, 1, 1] + grads[:, 2, 2]
        strain = 0.5 * (grads + jnp.swapaxes(grads, 1, 2))
        stress = (
            2.0 * shear_weight * strain
            + (lam_weight * trace_u)[:, None, None] * identity[None, :, :, None, None]
        )
        contrib = jnp.einsum("bkdij,cedbi->cebkj", smooth, stress, precision=HIGH)
        pooled = jnp.einsum("cebkj,bkq->ceqj", contrib, column_hot, precision=HIGH)
        own = pooled[:, :, :nblk]
        returned = send_back(pooled[:, :, nblk : nblk + ghosts], pooled[:, :, nblk + ghosts :])
        return alive * (own + returned) + KAPPA * field

    def curvature(first, second):
        return over_tiles(jnp.sum(first * second, axis=(1, 2, 3)))

    def squares(residual):
        return over_tiles(jnp.sum(residual * residual, axis=(1, 2, 3)))

    def over_tiles(x):
        size = lax.axis_size("tile")
        block = jnp.zeros((ROWS, LANES), F32).at[0, :cases].set(x)
        return jnp.sum(everywhere(block, size), axis=0)[0, :cases]

    def widen(scalars):
        return scalars[:, None, None, None]

    def run_solver(rhs):
        def sweep(i, state):
            solution, residual, direction, norm_now = state
            image = operate(direction)
            step_len = norm_now / curvature(direction, image)
            solution = solution + widen(step_len) * direction
            residual = residual - widen(step_len) * image
            norm_next = squares(residual)
            direction = residual + widen(norm_next / norm_now) * direction
            return solution, residual, direction, norm_next

        start = (jnp.zeros_like(rhs), rhs, rhs, squares(rhs))
        return lax.fori_loop(0, ITERS, sweep, start)[0]

    def phase(i, state):
        _, forward = state
        first = alive * load.reshape(field_shape)
        second = alive * (forward - target.reshape(field_shape))
        return forward, run_solver(jnp.where(i == 0, first, second))

    blank = jnp.zeros(field_shape, F32)
    forward, adjoint = lax.fori_loop(0, 2, phase, (blank, blank))
    grads = strains(jnp.concatenate([forward, adjoint], axis=0))
    grads_u = grads[:cases]
    grads_a = grads[cases:]
    trace_u = grads_u[:, 0, 0] + grads_u[:, 1, 1] + grads_u[:, 2, 2]
    trace_a = grads_a[:, 0, 0] + grads_a[:, 1, 1] + grads_a[:, 2, 2]
    strain_u = 0.5 * (grads_u + jnp.swapaxes(grads_u, 1, 2))
    strain_a = 0.5 * (grads_a + jnp.swapaxes(grads_a, 1, 2))
    local_lambda = (-weight * jnp.sum(trace_u * trace_a, axis=0)).reshape(-1)
    local_mu = (-2.0 * weight * jnp.sum(strain_u * strain_a, axis=(0, 1, 2))).reshape(-1)
    local = jnp.stack([local_lambda, local_mu])
    grad_lambda, grad_mu = local + lax.ppermute(local, "case", [(0, 1), (1, 0)])
    return (forward.reshape(load.shape), grad_lambda, grad_mu)


def shards(load, target, lame_lambda, lame_mu, volume, smooth, columns, send_list, counts):
    cases = load.shape[0]
    nblk = smooth.shape[0]
    ghosts = send_list.shape[2]
    pool_n = nblk + 2 * ghosts
    tiles, size = lax.axis_size("tile"), load.shape[2]
    place = lax.axis_index("tile").astype(jnp.int32).reshape(1)
    block = lambda n: arr(n, ROWS, LANES)
    wide = lambda n: arr(n, ROWS, 3 * LANES)
    tile8 = arr(ROWS, LANES)
    v_own, t_own, up, down, lam, shear, weight, mask, coef = call(
        functools.partial(prepare_body, nblk, ghosts),
        [block(nblk)] * 2 + [block(2 * ghosts + 1)] * 2 + [block(nblk)] * 3 + [tile8] * 2,
        [SM] * 3 + [pl.BlockSpec(memory_space=pltpu.HBM)] * 6,
        [pltpu.VMEM(x, F32) for x in ((3, cases, size), (3, cases, size), (size,), (size,), (size,), (1, 3, LANES, LANES))]
        + [pltpu.SemaphoreType.DMA((6,))],
    )(
        place, send_list, counts, in_hbm(load.transpose(1, 0, 2)), in_hbm(target.transpose(1, 0, 2)),
        in_hbm(lame_lambda), in_hbm(lame_mu), in_hbm(volume), in_hbm(smooth),
    )
    below = lax.ppermute(up, "tile", [(t, t + 1) for t in range(tiles - 1)])
    above = lax.ppermute(down, "tile", [(t + 1, t) for t in range(tiles - 1)])
    hops, step = [coef], 1
    while step < tiles:
        hops.append(hops[-1] + lax.ppermute(hops[-1], "tile", pairs_of(step, 0, tiles)))
        step *= 2
    coef = hops[-1]
    fwd, bwd = convert(smooth, hops[min(2, len(hops) - 1)])
    numbers = lambda x: x[2 * ghosts, 0, : Table.SIZE].astype(jnp.int32)
    table = (place, send_list, counts, numbers(below), numbers(above))
    matrix_scratch = pltpu.VMEM((pool_n, 3 * ROWS, LANES), BF16)
    pool_scratch = pltpu.VMEM((pool_n, ROWS, LANES), F32)
    side_scratch = pltpu.VMEM((nblk, ROWS, LANES), F32)
    msgs = [block(nblk)] + [block(2 * ghosts)] * 4
    scalars = [SM] * Table.NUMBER
    v0, t_pool, g0, gt, *rest, gram = call(
        functools.partial(first_body, nblk, ghosts),
        [block(pool_n)] * 2 + [wide(nblk)] * 2 + msgs + [tile8],
        [SM] + scalars + [VM] * 9,
        [matrix_scratch, matrix_scratch, pool_scratch],
    )(columns, *table, v_own, t_own, below, above, fwd, bwd, shear, lam, hops[min(3, len(hops) - 1)])

    def exchange(own, near, first, second, ghost, mask=mask):
        near = lax.ppermute(near, "tile", pairs_of(1, 0, tiles))
        first = lax.ppermute(first, "tile", pairs_of(2, 0, tiles))
        second = lax.ppermute(second, "tile", pairs_of(2, 2, tiles))
        relay = lax.ppermute(jnp.where(mask[None] > 0.0, first, second), "tile", pairs_of(1, 0, tiles))
        return own, ghost, near, relay, first, second

    def advance(j, basis, gram, rest):
        final = j == ITERS - 1
        ins = list(exchange(*rest))
        ins += list(basis) + [coef, gram, fwd, bwd, shear, lam]
        scratch = [matrix_scratch, pool_scratch, side_scratch, side_scratch]
        if not final:
            scratch.append(pool_scratch)
        return call(
            functools.partial(step_body, j, nblk, ghosts, final),
            [block(pool_n), wide(nblk)] + ([tile8] if final else [tile8] + msgs),
            [SM] + scalars + [VM] * len(ins),
            scratch,
        )(columns, *table, *ins)

    rest[1] = jnp.where(coef[None] > -1.0, rest[1], 0.0)
    basis, grads = [v0], [g0]
    for j in range(1, ITERS):
        v, g, gram, *rest = advance(j, basis, gram, rest)
        basis.append(v)
        grads.append(g)
    disp, gu, v0, g0, gram, worst, *rest = call(
        functools.partial(middle_body, nblk, ghosts, tiles),
        [arr(3, cases, size), wide(nblk), block(pool_n), wide(nblk), tile8, tile8] + msgs,
        [SM] + scalars + [VM] * (2 + 2 * ITERS + 6),
        [pool_scratch],
    )(columns, *table, everywhere(gram, tiles), coef, *basis, *grads, t_pool, gt, fwd, bwd, shear, lam)
    basis, grads = [v0], [g0]
    for j in range(1, ITERS):
        v, g, gram, *rest = advance(j, basis, gram, rest)
        basis.append(v)
        grads.append(g)
    out = call(
        functools.partial(final_body, nblk, tiles),
        [arr(2 * nblk + ROWS, LANES)],
        [VM] * (2 + ITERS + 3),
    )(everywhere(gram, tiles), coef, *grads, gu, weight, worst)[0]
    other = lax.ppermute(out, "case", [(0, 1), (1, 0)])
    grad_lambda, grad_mu, again = pl.pallas_call(
        functools.partial(closing_body, nblk),
        out_shape=[arr(size), arr(size), arr(1, dtype=jnp.int32)],
        in_specs=[VM, VM],
        out_specs=[VM, VM, SM],
        compiler_params=pltpu.CompilerParams(vmem_limit_bytes=LIMIT),
    )(out, other)
    return lax.cond(
        again[0] > 0,
        lambda: plain(load, target, lame_lambda, lame_mu, volume, smooth, columns, send_list, counts),
        lambda: (disp.transpose(1, 0, 2), grad_lambda, grad_mu),
    )


def solution(mesh):
    return jax.shard_map(
        shards,
        mesh=mesh,
        in_specs=(
            P("case", None, "tile"),
            P("case", None, "tile"),
            P("tile"),
            P("tile"),
            P("tile"),
            P("tile", None, None, None, None),
            P("tile", None),
            P("tile", None, None),
            P("tile"),
        ),
        out_specs=(P("case", None, "tile"), P("tile"), P("tile")),
        check_vma=False,
    )
```
